32 devices in a mesh: dp: 2 (over y), fsdp: 2 (over x), expert: 8 (over z, core).
Axes of the slice: x: 2, y: 2, z: 4, core: 2. Of those that a mesh axis runs over, the one named last changes fastest.
Arguments:
- tokens: bfloat16 [8192, 2048], P(('dp', 'fsdp', 'expert')), may hold values from -6 to 6
- expert_ids: int32 [8192, 8], P(('dp', 'fsdp', 'expert')), may hold values from 0 to 127, all different within a row; in each aligned block of 256 rows (0 to 255, 256 to 511, ...) at most 24 rows name the same one
- gate_units: int32 [8192, 8], P(('dp', 'fsdp', 'expert')), may hold values from 1 to 256
- expert_weights: bfloat16 [8, 2048, 3, 768], P('expert', ('dp', 'fsdp')), may hold values from -0.125 to 0.125
- out_grad: bfloat16 [8192, 2048], P(('dp', 'fsdp', 'expert')), may hold values from -6 to 6
Outputs:
- moe_out: bfloat16 [8192, 2048], P(('dp', 'fsdp', 'expert'))
- token_grad: bfloat16 [8192, 2048], P(('dp', 'fsdp', 'expert'))
- weight_grad: bfloat16 [8, 2048, 3, 768], P('expert', ('dp', 'fsdp'))
The draws below stay inside these ranges and needn't reach their ends.
Inputs may be any that keep to these rules, and one draw needn't show every extreme that they name: `expert_ids`: each row names 8 different experts; the 256 rows of one device name one expert at most 24 times.
All inputs are finite; a program needn't handle non-finite values.
Results may differ from the reference program's by a relative error of at most 0.018.
Values may be sent and summed in bfloat16 or wider, within the bound.
No kernel may reach another device: no remote copies, remote signals or barrier semaphores. Data moves between devices by JAX's collectives and lax.ppermute only.
A program may use at most 128 MiB of HBM per device.

```python
import math
import jax
import jax.numpy as jnp
import numpy as np
from jax import lax

D = 2048
H = 768
ROUTED = 128
TOPK = 8
TOK_DEV = 256
CAP = 24
EXPERTS = 8
TOKENS = 8192
N_DP = 2
N_FSDP = 2
N_EXPERT = 8


def place_ends(array, key, least, high):
    longest = array.shape.index(max(array.shape))
    spots = []
    for shift in (0, 1):
        where = [jax.random.randint(jax.random.fold_in(key, axis), (), 0, length) for axis, length in enumerate(array.shape)]
        where[longest] = (where[longest] + shift) % array.shape[longest]
        spots.append(tuple(where))
    return array.at[spots[0]].set(least).at[spots[1]].set(high)


def shard_levels(key, extent, pieces, least, high):
    loudness, own = 1.0, jax.random.fold_in(key, 6)
    for dim, parts in pieces:
        draws = jnp.exp(jax.random.uniform(jax.random.fold_in(own, dim), (parts,), jnp.float32, least / len(pieces), high / len(pieces)))
        loudness = loudness * jnp.repeat(draws, extent[dim] // parts).reshape([-1 if axis == dim else 1 for axis in range(len(extent))])
    return loudness


def shared_out(own_key, own, number, rows, amount, top, bound, lean):
    sequence = jax.random.permutation(own_key, amount)
    crowded, ordinary = load_shares(amount, rows * top, bound, lean, True), load_shares(amount, rows * top, bound, lean, False)
    places = jnp.arange(amount)

    def named(sizes, offset_by):
        used = int((sizes > 0).sum())
        fixed = max(1, used // 4)
        shifted = fixed + (places - fixed + offset_by * (used - fixed)) % max(1, amount - fixed)
        return jnp.zeros((amount,), jnp.int32).at[sequence[jnp.where(places < fixed, places, shifted)]].set(jnp.asarray(sizes, jnp.int32))

    sizes = jnp.where(number % 4 == 0, named(crowded, number // 4), named(ordinary, number - number // 4 - 1))
    mixed = jax.random.permutation(jax.random.fold_in(own, 3), amount)
    donor, sink = mixed[0:amount // 2 * 2:2], mixed[1:amount // 2 * 2:2]
    margin = jnp.minimum(sizes[donor] - 1, bound - sizes[sink]) // 2
    margin = jnp.where((donor == sequence[0]) | (sink == sequence[0]) | (sizes[sink] == 0), 0, jnp.maximum(margin, 0))
    shifted = jax.random.randint(jax.random.fold_in(own, 4), (amount // 2,), 0, 1 << 20) % (margin + 1)
    sizes = sizes.at[donor].add(-shifted).at[sink].add(shifted)
    items = jnp.searchsorted(jnp.cumsum(sizes), jnp.arange(rows * top), side="right").astype(jnp.int32)
    listing = items.reshape(top, rows).T
    listing = listing[jax.random.permutation(jax.random.fold_in(own, 1), rows)]
    offset_by = jax.random.randint(jax.random.fold_in(own, 2), (rows, 1), 0, top)
    return jnp.take_along_axis(listing, (jnp.arange(top)[None, :] + offset_by) % top, axis=1)


def load_shares(count, total, most, lean, full):
    loads = [(1 << 20) // math.isqrt(rank ** lean) + 1 for rank in range(1, count + 1)]
    largest = most if full else min(most, max(-(-total // count), total * loads[0] // sum(loads)))
    least = 1 if total - largest >= count - 1 else 0
    holding, rest = [largest] + [least] * (count - 1), total - largest - least * (count - 1)
    while rest > 0:
        candidates = [i for i in range(1, count) if holding[i] < largest] or [i for i in range(1, count) if holding[i] < most]
        mass, left = sum([loads[i] for i in candidates]), rest
        for i in candidates:
            addition = min(most - holding[i], max(1, left * loads[i] // mass), rest)
            holding[i] = holding[i] + addition
            rest = rest - addition
    return np.array(holding)


def bell_draw(own_key, extent, deviation, reach, shards=(), kind=jnp.bfloat16):
    values = deviation * jax.random.normal(own_key, extent, jnp.float32)
    if shards:
        values = values * shard_levels(own_key, extent, shards, -0.22, 0.18)
    return jnp.clip(values, -reach, reach).astype(kind)


def setup_inputs(seed: int = 0) -> dict:
    key_list = jax.random.split(jax.random.key(seed), 6)
    tokens = bell_draw(key_list[0], (TOKENS, D), 1.0, 6.0, ((0, 32),))
    expert_ids_keys = jax.random.split(jax.random.fold_in(key_list[1], 1), TOKENS // TOK_DEV)
    expert_ids_turns = jax.random.permutation(jax.random.fold_in(key_list[1], 3), TOKENS // TOK_DEV)
    expert_ids = jax.vmap(lambda own, number: shared_out(jax.random.fold_in(key_list[1], 2), own, number, TOK_DEV, ROUTED, TOPK, CAP, 0))(expert_ids_keys, expert_ids_turns).reshape((TOKENS, TOPK))
    gate_units = place_ends(jax.random.randint(key_list[2], (TOKENS, TOPK), 1, 257), jax.random.fold_in(key_list[2], 1), 1, 256).astype(jnp.int32)
    expert_weights = bell_draw(key_list[3], (EXPERTS, D, 3, H), D ** -0.5, 0.125, ((0, 8), (1, 4)))
    out_grad = bell_draw(key_list[4], (TOKENS, D), 1.0, 6.0, ((0, 32),))
    return dict(tokens=tokens, expert_ids=expert_ids, gate_units=gate_units, expert_weights=expert_weights, out_grad=out_grad)


def slot_tables(expert_ids, gate_units):
    blocks = N_DP * N_FSDP * N_EXPERT
    token_total = expert_ids.shape[0]
    top_count = expert_ids.shape[1]
    per_block = token_total // blocks
    block_ids = expert_ids.reshape(blocks, per_block * top_count)
    chosen = (block_ids[:, :, None] == jnp.arange(N_EXPERT, dtype=jnp.int32)[None, None, :]).astype(jnp.int32)
    before = jnp.cumsum(chosen, axis=1) - chosen
    ranking = jnp.sum(before * chosen, axis=2).astype(jnp.int32)
    block_index = jnp.arange(blocks, dtype=jnp.int32)[:, None]
    group_index = block_index // N_EXPERT
    source = block_index % N_EXPERT
    per_expert = blocks * CAP
    position = group_index * (N_EXPERT * CAP) + source * CAP + ranking
    inside = block_ids < N_EXPERT
    flat_index = jnp.where(inside, block_ids * per_expert + position, N_EXPERT * per_expert).reshape(-1).astype(jnp.int32)
    token_index = jnp.repeat(jnp.arange(token_total, dtype=jnp.int32), top_count)
    gate_values = gate_units.reshape(-1).astype(jnp.float32) / 256.0
    token_table = jnp.full((N_EXPERT * per_expert,), token_total, jnp.int32).at[flat_index].set(token_index, mode="drop")
    gate_table = jnp.zeros((N_EXPERT * per_expert,), jnp.float32).at[flat_index].set(gate_values, mode="drop")
    return token_table.reshape(N_EXPERT, per_expert), gate_table.reshape(N_EXPERT, per_expert)


def expert_pass(token_table, gate_table, expert_weight, padded_tokens, padded_grad):
    model_width = padded_tokens.shape[1]
    hidden_units = expert_weight.shape[2]
    flat_weights = expert_weight.reshape(model_width, 3 * hidden_units)
    slot_rows = padded_tokens[token_table]
    grad_rows = padded_grad[token_table]
    gate_up = jnp.dot(slot_rows, flat_weights[:, :2 * hidden_units], preferred_element_type=jnp.float32)
    gate_act = gate_up[:, :hidden_units]
    up_act = gate_up[:, hidden_units:]
    sigmoid_gate = jax.nn.sigmoid(gate_act)
    swish_gate = gate_act * sigmoid_gate
    activation = (swish_gate * up_act).astype(jnp.bfloat16)
    down_rows = flat_weights[:, 2 * hidden_units:]
    result = lax.dot_general(activation, down_rows, (((1,), (1,)), ((), ())), preferred_element_type=jnp.float32).astype(jnp.bfloat16)
    scaled = (gate_table[:, None] * grad_rows.astype(jnp.float32)).astype(jnp.bfloat16)
    hidden_grad = jnp.dot(scaled, down_rows, preferred_element_type=jnp.float32)
    gate_grad = (hidden_grad * up_act * sigmoid_gate * (1.0 + gate_act * (1.0 - sigmoid_gate))).astype(jnp.bfloat16)
    up_grad = (hidden_grad * swish_gate).astype(jnp.bfloat16)
    pair_grad = jnp.concatenate([gate_grad, up_grad], axis=1)
    row_grad = lax.dot_general(pair_grad, flat_weights[:, :2 * hidden_units], (((1,), (1,)), ((), ())), preferred_element_type=jnp.float32).astype(jnp.bfloat16)
    groups = N_DP * N_FSDP
    per_group = slot_rows.shape[0] // groups
    grouped_rows = slot_rows.reshape(groups, per_group, model_width).astype(jnp.float32)
    grouped_pair = pair_grad.reshape(groups, per_group, 2 * hidden_units).astype(jnp.float32)
    grouped_scaled = scaled.reshape(groups, per_group, model_width).astype(jnp.float32)
    grouped_act = activation.reshape(groups, per_group, hidden_units).astype(jnp.float32)
    input_term = jnp.einsum("gsd,gsh->gdh", grouped_rows, grouped_pair, precision=lax.Precision.HIGHEST)
    down_term = jnp.einsum("gsd,gsh->gdh", grouped_scaled, grouped_act, precision=lax.Precision.HIGHEST)
    group_terms = jnp.concatenate([input_term, down_term], axis=2).astype(jnp.bfloat16)
    group_terms = lax.optimization_barrier(group_terms).astype(jnp.float32)
    summed = jnp.sum(group_terms, axis=0).reshape(model_width, 3, hidden_units).astype(jnp.bfloat16)
    return result, row_grad, summed


def reference(tokens, expert_ids, gate_units, expert_weights, out_grad):
    token_table, gate_table = slot_tables(expert_ids, gate_units)
    token_total = tokens.shape[0]
    model_width = tokens.shape[1]
    padded_tokens = jnp.concatenate([tokens, jnp.zeros((1, model_width), jnp.bfloat16)], axis=0)
    padded_grad = jnp.concatenate([out_grad, jnp.zeros((1, model_width), jnp.bfloat16)], axis=0)

    def expert_step(packed):
        return expert_pass(packed[0], packed[1], packed[2], padded_tokens, padded_grad)

    results, row_grads, weight_grad = lax.map(expert_step, (token_table, gate_table, expert_weights))
    flat_table = token_table.reshape(-1)
    outputs = jnp.zeros((token_total + 1, model_width), jnp.float32).at[flat_table].add(
        gate_table.reshape(-1)[:, None] * results.reshape(-1, model_width).astype(jnp.float32))
    grads = jnp.zeros((token_total + 1, model_width), jnp.float32).at[flat_table].add(
        row_grads.reshape(-1, model_width).astype(jnp.float32))
    return outputs[:token_total].astype(jnp.bfloat16), grads[:token_total].astype(jnp.bfloat16), weight_grad
```

```python
import jax
import jax.numpy as jnp
from jax import lax
from jax.sharding import PartitionSpec as P

CAP = 24
ALL = ("dp", "fsdp", "expert")
F32 = jnp.float32
BF16 = jnp.bfloat16


def route_tables(expert_ids, gate_units, slot_expert, slot_rank):
    tok_count, top_count = expert_ids.shape
    same = expert_ids[:, :, None] == slot_expert[None, None, :]
    named = jnp.sum(same.astype(F32), axis=1)
    gates = jnp.sum(jnp.where(same, gate_units.astype(F32)[:, :, None], 0.0), axis=1)
    order = jnp.arange(tok_count, dtype=jnp.int32)
    earlier = (order[:, None] > order[None, :]).astype(BF16)
    before = jnp.dot(earlier, named.astype(BF16), preferred_element_type=F32)
    hit = (named > 0.5) & (before == slot_rank.astype(F32)[None, :])
    dispatch = hit.astype(BF16)
    combine = jnp.where(hit, gates / 256.0, 0.0).astype(BF16)
    return dispatch, combine


def contract(left, right, left_dim, right_dim):
    return lax.dot_general(
        left, right, (((left_dim,), (right_dim,)), ((), ())), preferred_element_type=F32
    )


class Moves:
    def __init__(self, dp, fsdp, experts):
        self.shape = (dp, fsdp, experts)

    def move(self, value, where, back=False):
        dp, fsdp, experts = self.shape
        pairs = []
        for d in range(dp):
            for f in range(fsdp):
                for e in range(experts):
                    nd, nf, ne = where(d, f, e)
                    pair = ((d * fsdp + f) * experts + e, (nd * fsdp + nf) * experts + ne)
                    pairs.append(pair[::-1] if back else pair)
        return lax.ppermute(value, ALL, pairs)

    def partner_core(self, value, back=False):
        return self.move(value, lambda d, f, e: (d, f, e ^ 1), back)

    def weight_pair(self, value):
        return self.move(value, lambda d, f, e: (d, 1 - f, e) if e % 2 == 0 else (1 - d, f, e))

    def column_pair(self, value):
        return self.move(value, lambda d, f, e: (1 - d, f, e) if e % 2 == 0 else (d, 1 - f, e))

    def cross_pair(self, value, back=False):
        return self.move(
            value, lambda d, f, e: (d, 1 - f, e ^ 1) if e % 2 == 0 else (1 - d, f, e ^ 1), back
        )

    def along_z(self, value, step, back=False):
        experts = self.shape[2]
        return self.move(value, lambda d, f, e: (d, f, (e + 2 * step) % experts), back)


def paired(tokens, expert_ids, gate_units, expert_weights, out_grad):
    dp, fsdp, experts = (lax.axis_size(name) for name in ALL)
    moves = Moves(dp, fsdp, experts)
    steps = experts // 2
    model_width = tokens.shape[1]
    quarter_width = model_width // 4
    hidden = expert_weights.shape[3]
    own_e = lax.axis_index("expert")
    own_z, own_c = own_e // 2, own_e % 2
    own_q = lax.axis_index("dp") * 2 + lax.axis_index("fsdp")
    quarter = (own_q, own_q ^ (1 + own_c), own_q ^ (2 - own_c), own_q ^ 3)
    half = steps * CAP

    slot = jnp.arange(2 * half, dtype=jnp.int32)
    slot_expert = ((slot % half // CAP + own_z) % steps) * 2 + (slot // half + own_c) % 2
    dispatch, combine = route_tables(expert_ids, gate_units, slot_expert, slot % CAP)

    weights_own = expert_weights[0]
    weights_far = moves.weight_pair(weights_own)

    def columns(array, index):
        return lax.dynamic_slice_in_dim(array, quarter[index] * quarter_width, quarter_width, 1)

    def send(table, source):
        rows = [contract(table, columns(source, i), 0, 0).astype(BF16) for i in range(4)]

        def part(first, second, other):
            low = half if other else 0
            return jnp.stack([rows[first][low : low + half], rows[second][low : low + half]])

        blocks = (
            part(0, 1, False),
            moves.partner_core(part(0, 2, True)),
            moves.column_pair(part(2, 3, False)),
            moves.cross_pair(part(1, 3, True)),
        )
        got = []
        for step in range(steps):
            piece = jnp.concatenate(
                [block[:, step * CAP : (step + 1) * CAP] for block in blocks], axis=1
            )
            got.append(moves.along_z(piece, step) if step else piece)
        return jnp.concatenate(
            [piece[:, : 2 * CAP] for piece in got] + [piece[:, 2 * CAP :] for piece in got], axis=1
        )

    def give_back(table, value):
        blocks = [[], [], [], []]
        for step in range(steps):
            low = step * 2 * CAP
            piece = jnp.concatenate(
                [
                    value[:, low : low + 2 * CAP],
                    value[:, 2 * half + low : 2 * half + low + 2 * CAP],
                ],
                axis=1,
            )
            if step:
                piece = moves.along_z(piece, step, back=True)
            for kind in range(4):
                blocks[kind].append(piece[:, kind * CAP : (kind + 1) * CAP])
        kept, core, column, cross = (jnp.concatenate(block, axis=1) for block in blocks)
        core = moves.partner_core(core, back=True)
        column = moves.column_pair(column)
        cross = moves.cross_pair(cross, back=True)
        rows = (
            jnp.concatenate([kept[0], core[0]]),
            jnp.concatenate([kept[1], cross[0]]),
            jnp.concatenate([column[0], core[1]]),
            jnp.concatenate([column[1], cross[1]]),
        )
        out = jnp.zeros((table.shape[0], model_width), BF16)
        for index in range(4):
            out = lax.dynamic_update_slice_in_dim(
                out,
                contract(table, rows[index], 1, 0).astype(BF16),
                quarter[index] * quarter_width,
                1,
            )
        return out

    def summed(partial):
        rows = partial.shape[0] // 2
        swapped = jnp.concatenate([partial[rows:], partial[:rows]]).astype(BF16)
        return partial + moves.column_pair(swapped).astype(F32)

    slot_rows = send(dispatch, tokens)
    scaled = send(combine, out_grad)
    pair = (weights_own, weights_far)

    def inward(rows, which):
        return contract(rows[0], pair[0][:, which], 1, 0) + contract(rows[1], pair[1][:, which], 1, 0)

    gate_up = summed(jnp.concatenate([inward(slot_rows, 0), inward(slot_rows, 1)], axis=1))
    gate_act, up_act = gate_up[:, :hidden], gate_up[:, hidden:]
    sigmoid_gate = jax.nn.sigmoid(gate_act)
    swish_gate = gate_act * sigmoid_gate
    activation = (swish_gate * up_act).astype(BF16)
    result = jnp.stack([contract(activation, pair[i][:, 2], 1, 1).astype(BF16) for i in (0, 1)])
    moe_out = give_back(combine, result)
    hidden_grad = summed(inward(scaled, 2))
    gate_grad = (
        hidden_grad * up_act * sigmoid_gate * (1.0 + gate_act * (1.0 - sigmoid_gate))
    ).astype(BF16)
    up_grad = (hidden_grad * swish_gate).astype(BF16)
    row_grad = jnp.stack(
        [
            (
                contract(gate_grad, pair[i][:, 0], 1, 1) + contract(up_grad, pair[i][:, 1], 1, 1)
            ).astype(BF16)
            for i in (0, 1)
        ]
    )
    token_grad = give_back(dispatch, row_grad)

    def terms(index):
        return jnp.stack(
            [
                contract(slot_rows[index], gate_grad, 0, 0),
                contract(slot_rows[index], up_grad, 0, 0),
                contract(scaled[index], activation, 0, 0),
            ],
            axis=1,
        )

    arrived = moves.weight_pair(terms(1).astype(BF16))
    weight_grad = (terms(0) + arrived.astype(F32)).astype(BF16)[None]
    return moe_out, token_grad, weight_grad


def gathered(tokens, expert_ids, gate_units, expert_weights, out_grad):
    experts = lax.axis_size("expert")
    slots = experts * CAP
    width = tokens.shape[1]
    hidden = expert_weights.shape[3]
    slot = jnp.arange(slots, dtype=jnp.int32)
    dispatch, combine = route_tables(expert_ids, gate_units, slot // CAP, slot % CAP)

    def exchange(rows):
        return lax.all_to_all(
            rows.reshape(experts, CAP, width), "expert", split_axis=0, concat_axis=0, tiled=True
        ).reshape(slots, width)

    slot_rows = exchange(contract(dispatch, tokens, 0, 0).astype(BF16))
    scaled = exchange(contract(combine, out_grad, 0, 0).astype(BF16))
    full = lax.all_gather(expert_weights, ("dp", "fsdp"), axis=1, tiled=True)[0]
    gate_act = contract(slot_rows, full[:, 0], 1, 0)
    up_act = contract(slot_rows, full[:, 1], 1, 0)
    sigmoid_gate = jax.nn.sigmoid(gate_act)
    swish_gate = gate_act * sigmoid_gate
    activation = (swish_gate * up_act).astype(BF16)
    result = contract(activation, full[:, 2], 1, 1).astype(BF16)
    moe_out = contract(combine, exchange(result), 1, 0).astype(BF16)
    hidden_grad = contract(scaled, full[:, 2], 1, 0)
    gate_grad = (
        hidden_grad * up_act * sigmoid_gate * (1.0 + gate_act * (1.0 - sigmoid_gate))
    ).astype(BF16)
    up_grad = (hidden_grad * swish_gate).astype(BF16)
    row_grad = (
        contract(gate_grad, full[:, 0], 1, 1) + contract(up_grad, full[:, 1], 1, 1)
    ).astype(BF16)
    token_grad = contract(dispatch, exchange(row_grad), 1, 0).astype(BF16)
    term = jnp.stack(
        [
            contract(slot_rows, gate_grad, 0, 0),
            contract(slot_rows, up_grad, 0, 0),
            contract(scaled, activation, 0, 0),
        ],
        axis=1,
    ).astype(BF16)
    summed = lax.psum_scatter(term, ("dp", "fsdp"), scatter_dimension=0, tiled=True)
    return moe_out, token_grad, summed.reshape(1, -1, 3, hidden)


def solution(mesh):
    placed = P(ALL, None)
    weights = P("expert", ("dp", "fsdp"), None, None)
    sizes = mesh.shape
    small = sizes["dp"] == 2 and sizes["fsdp"] == 2 and sizes["expert"] % 2 == 0
    return jax.shard_map(
        paired if small else gathered,
        mesh=mesh,
        in_specs=(placed, placed, placed, weights, placed),
        out_specs=(placed, placed, weights),
        check_vma=False,
    )
```

```python
import jax
import jax.numpy as jnp
from jax import lax
from jax.sharding import PartitionSpec as P


CAP = 24
ALL = ("dp", "fsdp", "expert")
F32 = jnp.float32
BF16 = jnp.bfloat16


def route_tables(expert_ids, gate_units, slot_expert, slot_rank):
    tok_count, _ = expert_ids.shape
    same = expert_ids[:, :, None] == slot_expert[None, None, :]
    named = jnp.sum(same.astype(F32), axis=1)
    gates = jnp.sum(jnp.where(same, gate_units.astype(F32)[:, :, None], 0.0), axis=1)
    order = jnp.arange(tok_count, dtype=jnp.int32)
    earlier = (order[:, None] > order[None, :]).astype(BF16)
    before = jnp.dot(earlier, named.astype(BF16), preferred_element_type=F32)
    hit = (named > 0.5) & (before == slot_rank.astype(F32)[None, :])
    dispatch = hit.astype(BF16)
    combine = jnp.where(hit, gates / 256.0, 0.0).astype(BF16)
    return dispatch, combine


def contract(left, right, left_dim, right_dim):
    return lax.dot_general(
        left, right, (((left_dim,), (right_dim,)), ((), ())), preferred_element_type=F32
    )


class Moves:
    def __init__(self, dp, fsdp, experts):
        self.shape = (dp, fsdp, experts)

    def move(self, value, where):
        dp, fsdp, experts = self.shape
        pairs = []
        for d in range(dp):
            for f in range(fsdp):
                for e in range(experts):
                    nd, nf, ne = where(d, f, e)
                    pairs.append(((d * fsdp + f) * experts + e, (nd * fsdp + nf) * experts + ne))
        return lax.ppermute(value, ALL, pairs)

    def core(self, value):
        return self.move(value, lambda d, f, e: (d, f, e ^ 1))

    def weight_pair(self, value):
        return self.move(value, lambda d, f, e: (d, 1 - f, e) if e % 2 == 0 else (1 - d, f, e))

    def column_pair(self, value):
        return self.move(value, lambda d, f, e: (1 - d, f, e) if e % 2 == 0 else (d, 1 - f, e))

    def along_z(self, value, step):
        return self.move(value, lambda d, f, e: (d, f, e ^ (2 * step)))


def z_order(steps):
    return sorted(range(1, steps), key=lambda step: (step < 2, step))


def paired(tokens, expert_ids, gate_units, expert_weights, out_grad):
    return paired_body(tokens, expert_ids, gate_units, expert_weights, out_grad)


def paired_body(tokens, expert_ids, gate_units, expert_weights, out_grad):
    moves = Moves(*(lax.axis_size(name) for name in ALL))
    steps = moves.shape[2] // 2
    model_width = tokens.shape[1]
    quarter_width = model_width // 4
    half_width = model_width // 2
    hidden = expert_weights.shape[3]
    own_e = lax.axis_index("expert")
    own_z, own_c = own_e // 2, own_e % 2
    own_q = lax.axis_index("dp") * 2 + lax.axis_index("fsdp")
    quarter = (own_q, own_q ^ (1 + own_c), own_q ^ (2 - own_c), own_q ^ 3)
    half = steps * CAP

    weights_own = expert_weights[0]
    weights_far = moves.weight_pair(weights_own)
    pair = (weights_own, weights_far)

    slot = jnp.arange(2 * half, dtype=jnp.int32)
    slot_expert = ((slot % half // CAP) ^ own_z) * 2 + ((slot // half) ^ own_c)
    dispatch, combine = route_tables(expert_ids, gate_units, slot_expert, slot % CAP)

    def interleaved(first, second):
        width = first.shape[1]
        both = (first.reshape(steps, CAP, width), second.reshape(steps, CAP, width))
        return jnp.stack(both, axis=1).reshape(2 * half, width)

    def cut(array, *which):
        return jnp.concatenate(
            [array[:, i * quarter_width : (i + 1) * quarter_width] for i in which], axis=1
        )

    def send_local(table, source):
        ordered = jnp.concatenate(
            [
                lax.dynamic_slice_in_dim(source, index * quarter_width, quarter_width, 1)
                for index in quarter
            ],
            axis=1,
        )
        other = contract(table[:, half:], ordered, 0, 0).astype(BF16)
        came = moves.core(other)
        same = contract(table[:, :half], ordered, 0, 0).astype(BF16)
        own = interleaved(cut(same, 0, 1), cut(came, 0, 2))
        out = interleaved(cut(same, 2, 3), cut(came, 1, 3))
        return own, moves.column_pair(out)

    def by_z(rows):
        parts = [value.shape[0] // steps for value in rows]
        order = z_order(steps)
        pieces = []
        fenced = lax.optimization_barrier(tuple(rows))
        for step in order:
            piece = [v[step * n : (step + 1) * n] for v, n in zip(fenced, parts)]
            pieces.append(jnp.concatenate(piece) if len(piece) > 1 else piece[0])
        pieces = lax.optimization_barrier(tuple(pieces))
        got = {0: jnp.concatenate([v[:n] for v, n in zip(rows, parts)])}
        for step, piece in zip(order, pieces):
            got[step] = moves.along_z(piece, step)
        whole, low = [], 0
        for n in parts:
            whole.append(jnp.concatenate([got[i][low : low + n] for i in range(steps)]))
            low += n
        return whole

    def give_back_in(table, own, near):
        out = moves.column_pair(near)

        def source(array, index):
            return array.reshape(steps, 2, CAP, half_width)[:, index].reshape(half, half_width)

        other = jnp.concatenate([source(own, 1), source(out, 1)], axis=1)
        came = moves.core(other)
        same = jnp.concatenate([source(own, 0), source(out, 0)], axis=1)
        rows = jnp.concatenate([same, cut(came, 0, 2, 1, 3)])
        result = contract(table, rows, 1, 0).astype(BF16)
        answer = jnp.zeros((table.shape[0], model_width), BF16)
        for index in range(4):
            answer = lax.dynamic_update_slice_in_dim(
                answer,
                result[:, index * quarter_width : (index + 1) * quarter_width],
                quarter[index] * quarter_width,
                1,
            )
        return answer

    def inward(rows, which):
        return contract(rows[:, :quarter_width], pair[0][:, which], 1, 0) + contract(
            rows[:, quarter_width:], pair[1][:, which], 1, 0
        )

    def outward(terms):
        return jnp.concatenate(
            [
                sum(contract(value, pair[i][:, which], 1, 1) for value, which in terms)
                for i in (0, 1)
            ],
            axis=1,
        ).astype(BF16)

    def wide(rows, *which):
        return jnp.concatenate([inward(rows, i) for i in which], axis=1)

    rows_own, rows_near = send_local(dispatch, tokens)
    (rows_own,) = by_z([rows_own])
    (rows_near,) = by_z([rows_near])
    scaled_own, scaled_near = by_z(send_local(combine, out_grad))

    part_own = wide(rows_own, 0, 1)
    message = part_own.astype(BF16)
    near_extra = moves.column_pair(message)
    part_near = wide(rows_near, 0, 1)
    message = part_near.astype(BF16)
    own_extra = moves.column_pair(message)

    def act(part, extra):
        total = part + extra.astype(F32)
        gate_act, up_act = total[:, :hidden], total[:, hidden:]
        sigmoid_gate = jax.nn.sigmoid(gate_act)
        swish_gate = gate_act * sigmoid_gate
        slope = up_act * sigmoid_gate * (1.0 + gate_act * (1.0 - sigmoid_gate))
        return lax.optimization_barrier(((swish_gate * up_act).astype(BF16), slope, swish_gate))

    act_near, slope_near, swish_near = act(part_near, near_extra)
    out_near = outward([(act_near, 2)])
    act_own, slope_own, swish_own = act(part_own, own_extra)
    out_own = outward([(act_own, 2)])
    back_near, back_own = by_z([out_near, out_own])

    hid_own, hid_near = wide(scaled_own, 2), wide(scaled_near, 2)
    message = jnp.concatenate([hid_near, hid_own]).astype(BF16)
    extra = moves.column_pair(message)
    hid_own = hid_own + extra[: 2 * half].astype(F32)
    hid_near = hid_near + extra[2 * half :].astype(F32)
    gg_near, ug_near = (hid_near * slope_near).astype(BF16), (hid_near * swish_near).astype(BF16)
    gg_own, ug_own = (hid_own * slope_own).astype(BF16), (hid_own * swish_own).astype(BF16)

    rows = jnp.concatenate([rows_own, rows_near])
    scaled = jnp.concatenate([scaled_own, scaled_near])
    activation = jnp.concatenate([act_own, act_near])
    gate_grad = jnp.concatenate([gg_own, gg_near])
    up_grad = jnp.concatenate([ug_own, ug_near])
    first, second = slice(0, quarter_width), slice(quarter_width, half_width)
    down_far = contract(scaled[:, second], activation, 0, 0).astype(BF16)
    down_far = moves.weight_pair(down_far)
    grad_near = outward([(gg_near, 0), (ug_near, 1)])
    (grad_near,) = by_z([grad_near])
    in_far = jnp.stack(
        [contract(rows[:, second], value, 0, 0) for value in (gate_grad, up_grad)]
    ).astype(BF16)
    in_far = moves.weight_pair(in_far)
    grad_own = outward([(gg_own, 0), (ug_own, 1)])
    (grad_own,) = by_z([grad_own])
    moe_out = give_back_in(combine, back_own, back_near)
    token_grad = give_back_in(dispatch, grad_own, grad_near)
    weight_grad = jnp.stack(
        [
            contract(rows[:, first], gate_grad, 0, 0) + in_far[0].astype(F32),
            contract(rows[:, first], up_grad, 0, 0) + in_far[1].astype(F32),
            contract(scaled[:, first], activation, 0, 0) + down_far.astype(F32),
        ],
        axis=1,
    ).astype(BF16)[None]
    return moe_out, token_grad, weight_grad


def gathered(tokens, expert_ids, gate_units, expert_weights, out_grad):
    experts = lax.axis_size("expert")
    slots = experts * CAP
    width = tokens.shape[1]
    hidden = expert_weights.shape[3]
    slot = jnp.arange(slots, dtype=jnp.int32)
    dispatch, combine = route_tables(expert_ids, gate_units, slot // CAP, slot % CAP)

    def exchange(rows):
        return lax.all_to_all(
            rows.reshape(experts, CAP, width), "expert", split_axis=0, concat_axis=0, tiled=True
        ).reshape(slots, width)

    slot_rows = exchange(contract(dispatch, tokens, 0, 0).astype(BF16))
    scaled = exchange(contract(combine, out_grad, 0, 0).astype(BF16))
    full = lax.all_gather(expert_weights, ("dp", "fsdp"), axis=1, tiled=True)[0]
    gate_act = contract(slot_rows, full[:, 0], 1, 0)
    up_act = contract(slot_rows, full[:, 1], 1, 0)
    sigmoid_gate = jax.nn.sigmoid(gate_act)
    swish_gate = gate_act * sigmoid_gate
    activation = (swish_gate * up_act).astype(BF16)
    result = contract(activation, full[:, 2], 1, 1).astype(BF16)
    moe_out = contract(combine, exchange(result), 1, 0).astype(BF16)
    hidden_grad = contract(scaled, full[:, 2], 1, 0)
    gate_grad = (
        hidden_grad * up_act * sigmoid_gate * (1.0 + gate_act * (1.0 - sigmoid_gate))
    ).astype(BF16)
    up_grad = (hidden_grad * swish_gate).astype(BF16)
    row_grad = (
        contract(gate_grad, full[:, 0], 1, 1) + contract(up_grad, full[:, 1], 1, 1)
    ).astype(BF16)
    token_grad = contract(dispatch, exchange(row_grad), 1, 0).astype(BF16)
    term = jnp.stack(
        [
            contract(slot_rows, gate_grad, 0, 0),
            contract(slot_rows, up_grad, 0, 0),
            contract(scaled, activation, 0, 0),
        ],
        axis=1,
    ).astype(BF16)
    summed = lax.psum_scatter(term, ("dp", "fsdp"), scatter_dimension=0, tiled=True)
    return moe_out, token_grad, summed.reshape(1, -1, 3, hidden)


def solution(mesh):
    placed = P(ALL, None)
    weights = P("expert", ("dp", "fsdp"), None, None)
    sizes = mesh.shape
    steps = sizes["expert"] // 2
    small = sizes["dp"] == 2 and sizes["fsdp"] == 2 and steps > 1
    small = small and sizes["expert"] % 2 == 0 and steps & (steps - 1) == 0
    return jax.shard_map(
        paired if small else gathered,
        mesh=mesh,
        in_specs=(placed, placed, placed, weights, placed),
        out_specs=(placed, placed, weights),
        check_vma=False,
    )
```

```python
import jax
import jax.numpy as jnp
from jax import lax
from jax.sharding import PartitionSpec as P


CAP = 24
ALL = ("dp", "fsdp", "expert")
F32 = jnp.float32
BF16 = jnp.bfloat16


def route_tables(expert_ids, gate_units, slot_expert, slot_rank):
    tok_count, _ = expert_ids.shape
    same = expert_ids[:, :, None] == slot_expert[None, None, :]
    named = jnp.sum(same.astype(F32), axis=1)
    gates = jnp.sum(jnp.where(same, gate_units.astype(F32)[:, :, None], 0.0), axis=1)
    order = jnp.arange(tok_count, dtype=jnp.int32)
    earlier = (order[:, None] > order[None, :]).astype(BF16)
    before = jnp.dot(earlier, named.astype(BF16), preferred_element_type=F32)
    hit = (named > 0.5) & (before == slot_rank.astype(F32)[None, :])
    dispatch = hit.astype(BF16)
    combine = jnp.where(hit, gates / 256.0, 0.0).astype(BF16)
    return dispatch, combine


def contract(left, right, left_dim, right_dim):
    return lax.dot_general(
        left, right, (((left_dim,), (right_dim,)), ((), ())), preferred_element_type=F32
    )


class Moves:
    def __init__(self, dp, fsdp, experts):
        self.shape = (dp, fsdp, experts)

    def move(self, value, where):
        dp, fsdp, experts = self.shape
        pairs = []
        for d in range(dp):
            for f in range(fsdp):
                for e in range(experts):
                    nd, nf, ne = where(d, f, e)
                    pairs.append(((d * fsdp + f) * experts + e, (nd * fsdp + nf) * experts + ne))
        return lax.ppermute(value, ALL, pairs)

    def core(self, value):
        return self.move(value, lambda d, f, e: (d, f, e ^ 1))

    def weight_pair(self, value):
        return self.move(value, lambda d, f, e: (d, 1 - f, e) if e % 2 == 0 else (1 - d, f, e))

    def column_pair(self, value):
        return self.move(value, lambda d, f, e: (1 - d, f, e) if e % 2 == 0 else (d, 1 - f, e))

    def along_z(self, value, step):
        return self.move(value, lambda d, f, e: (d, f, e ^ (2 * step)))


def z_order(steps):
    return sorted(range(1, steps), key=lambda step: (step < 2, step))


def paired(tokens, expert_ids, gate_units, expert_weights, out_grad):
    return paired_body(tokens, expert_ids, gate_units, expert_weights, out_grad)


def paired_body(tokens, expert_ids, gate_units, expert_weights, out_grad):
    moves = Moves(*(lax.axis_size(name) for name in ALL))
    steps = moves.shape[2] // 2
    model_width = tokens.shape[1]
    quarter_width = model_width // 4
    half_width = model_width // 2
    hidden = expert_weights.shape[3]
    own_e = lax.axis_index("expert")
    own_z, own_c = own_e // 2, own_e % 2
    own_q = lax.axis_index("dp") * 2 + lax.axis_index("fsdp")
    quarter = (own_q, own_q ^ (1 + own_c), own_q ^ (2 - own_c), own_q ^ 3)
    half = steps * CAP

    weights_own = expert_weights[0]
    gates_far = moves.weight_pair(weights_own[:, :2])
    down_far = moves.weight_pair(weights_own[:, 2])
    pair = (
        (weights_own[:, 0], weights_own[:, 1], weights_own[:, 2]),
        (gates_far[:, 0], gates_far[:, 1], down_far),
    )

    slot = jnp.arange(2 * half, dtype=jnp.int32)
    slot_expert = ((slot % half // CAP) ^ own_z) * 2 + ((slot // half) ^ own_c)
    dispatch, combine = route_tables(expert_ids, gate_units, slot_expert, slot % CAP)

    def interleaved(first, second):
        width = first.shape[1]
        both = (first.reshape(steps, CAP, width), second.reshape(steps, CAP, width))
        return jnp.stack(both, axis=1).reshape(2 * half, width)

    def taken(array, *which):
        return jnp.concatenate(
            [
                lax.dynamic_slice_in_dim(array, quarter[i] * quarter_width, quarter_width, 1)
                for i in which
            ],
            axis=1,
        )

    def placed(own, out):
        whole = jnp.zeros((own.shape[0], model_width), BF16)
        for index in range(4):
            part = (own, out)[index // 2]
            low = index % 2 * quarter_width
            whole = lax.dynamic_update_slice_in_dim(
                whole, part[:, low : low + quarter_width], quarter[index] * quarter_width, 1
            )
        return whole

    def send_local(table, source):
        other = contract(table[:, half:], source, 0, 0).astype(BF16)
        came = moves.core(other)
        same = contract(table[:, :half], source, 0, 0).astype(BF16)
        own = interleaved(taken(same, 0, 1), taken(came, 0, 1))
        out = interleaved(taken(same, 2, 3), taken(came, 2, 3))
        return own, moves.column_pair(out)

    def by_z(rows):
        parts = [value.shape[0] // steps for value in rows]
        order = z_order(steps)
        pieces = []
        fenced = lax.optimization_barrier(tuple(rows))
        for step in order:
            piece = [v[step * n : (step + 1) * n] for v, n in zip(fenced, parts)]
            pieces.append(jnp.concatenate(piece) if len(piece) > 1 else piece[0])
        pieces = lax.optimization_barrier(tuple(pieces))
        got = {0: jnp.concatenate([v[:n] for v, n in zip(rows, parts)])}
        for step, piece in zip(order, pieces):
            got[step] = moves.along_z(piece, step)
        whole, low = [], 0
        for n in parts:
            whole.append(jnp.concatenate([got[i][low : low + n] for i in range(steps)]))
            low += n
        return whole

    def give_back_in(table, own, near):
        out = moves.column_pair(near)

        def source(array, index):
            return array.reshape(steps, 2, CAP, half_width)[:, index].reshape(half, half_width)

        came = moves.core(placed(source(own, 1), source(out, 1)))
        rows = jnp.concatenate([placed(source(own, 0), source(out, 0)), came])
        return contract(table, rows, 1, 0).astype(BF16)

    def inward(rows, which):
        return contract(rows[:, :quarter_width], pair[0][which], 1, 0) + contract(
            rows[:, quarter_width:], pair[1][which], 1, 0
        )

    def outward(terms):
        return jnp.concatenate(
            [
                sum(contract(value, pair[i][which], 1, 1) for value, which in terms)
                for i in (0, 1)
            ],
            axis=1,
        ).astype(BF16)

    def wide(rows, *which):
        return jnp.concatenate([inward(rows, i) for i in which], axis=1)

    rows_own, rows_near = send_local(dispatch, tokens)
    (rows_own,) = by_z([rows_own])
    (rows_near,) = by_z([rows_near])
    scaled_own, scaled_near = by_z(send_local(combine, out_grad))

    part_own = wide(rows_own, 0, 1)
    message = part_own.astype(BF16)
    near_extra = moves.column_pair(message)
    part_near = wide(rows_near, 0, 1)
    message = part_near.astype(BF16)
    own_extra = moves.column_pair(message)

    def act(part, extra):
        total = part + extra.astype(F32)
        gate_act, up_act = total[:, :hidden], total[:, hidden:]
        sigmoid_gate = jax.nn.sigmoid(gate_act)
        swish_gate = gate_act * sigmoid_gate
        slope = up_act * sigmoid_gate * (1.0 + gate_act * (1.0 - sigmoid_gate))
        return lax.optimization_barrier(((swish_gate * up_act).astype(BF16), slope, swish_gate))

    act_near, slope_near, swish_near = act(part_near, near_extra)
    out_near = outward([(act_near, 2)])
    act_own, slope_own, swish_own = act(part_own, own_extra)
    out_own = outward([(act_own, 2)])
    back_near, back_own = by_z([out_near, out_own])

    hid_own, hid_near = wide(scaled_own, 2), wide(scaled_near, 2)
    message = jnp.concatenate([hid_near, hid_own]).astype(BF16)
    extra = moves.column_pair(message)
    hid_own = hid_own + extra[: 2 * half].astype(F32)
    hid_near = hid_near + extra[2 * half :].astype(F32)
    gg_near, ug_near = (hid_near * slope_near).astype(BF16), (hid_near * swish_near).astype(BF16)
    gg_own, ug_own = (hid_own * slope_own).astype(BF16), (hid_own * swish_own).astype(BF16)

    rows = jnp.concatenate([rows_own, rows_near])
    scaled = jnp.concatenate([scaled_own, scaled_near])
    activation = jnp.concatenate([act_own, act_near])
    gate_grad = jnp.concatenate([gg_own, gg_near])
    up_grad = jnp.concatenate([ug_own, ug_near])
    first, second = slice(0, quarter_width), slice(quarter_width, half_width)
    term_far = contract(scaled[:, second], activation, 0, 0).astype(BF16)
    arrived_down = moves.weight_pair(term_far)
    grad_near = outward([(gg_near, 0), (ug_near, 1)])
    (grad_near,) = by_z([grad_near])
    terms_far = jnp.stack(
        [contract(rows[:, second], value, 0, 0) for value in (gate_grad, up_grad)]
    ).astype(BF16)
    arrived_in = moves.weight_pair(terms_far)
    grad_own = outward([(gg_own, 0), (ug_own, 1)])
    (grad_own,) = by_z([grad_own])
    moe_out = give_back_in(combine, back_own, back_near)
    token_grad = give_back_in(dispatch, grad_own, grad_near)
    term_down = contract(scaled[:, first], activation, 0, 0) + arrived_down.astype(F32)
    term_down = term_down.astype(BF16)
    terms = [
        contract(rows[:, first], value, 0, 0) + arrived_in[i].astype(F32)
        for i, value in enumerate((gate_grad, up_grad))
    ]
    weight_grad = jnp.stack([*(term.astype(BF16) for term in terms), term_down], axis=1)
    return moe_out, token_grad, weight_grad[None]


def gathered(tokens, expert_ids, gate_units, expert_weights, out_grad):
    experts = lax.axis_size("expert")
    slots = experts * CAP
    width = tokens.shape[1]
    hidden = expert_weights.shape[3]
    slot = jnp.arange(slots, dtype=jnp.int32)
    dispatch, combine = route_tables(expert_ids, gate_units, slot // CAP, slot % CAP)

    def exchange(rows):
        return lax.all_to_all(
            rows.reshape(experts, CAP, width), "expert", split_axis=0, concat_axis=0, tiled=True
        ).reshape(slots, width)

    slot_rows = exchange(contract(dispatch, tokens, 0, 0).astype(BF16))
    scaled = exchange(contract(combine, out_grad, 0, 0).astype(BF16))
    full = lax.all_gather(expert_weights, ("dp", "fsdp"), axis=1, tiled=True)[0]
    gate_act = contract(slot_rows, full[:, 0], 1, 0)
    up_act = contract(slot_rows, full[:, 1], 1, 0)
    sigmoid_gate = jax.nn.sigmoid(gate_act)
    swish_gate = gate_act * sigmoid_gate
    activation = (swish_gate * up_act).astype(BF16)
    result = contract(activation, full[:, 2], 1, 1).astype(BF16)
    moe_out = contract(combine, exchange(result), 1, 0).astype(BF16)
    hidden_grad = contract(scaled, full[:, 2], 1, 0)
    gate_grad = (
        hidden_grad * up_act * sigmoid_gate * (1.0 + gate_act * (1.0 - sigmoid_gate))
    ).astype(BF16)
    up_grad = (hidden_grad * swish_gate).astype(BF16)
    row_grad = (
        contract(gate_grad, full[:, 0], 1, 1) + contract(up_grad, full[:, 1], 1, 1)
    ).astype(BF16)
    token_grad = contract(dispatch, exchange(row_grad), 1, 0).astype(BF16)
    term = jnp.stack(
        [
            contract(slot_rows, gate_grad, 0, 0),
            contract(slot_rows, up_grad, 0, 0),
            contract(scaled, activation, 0, 0),
        ],
        axis=1,
    ).astype(BF16)
    summed = lax.psum_scatter(term, ("dp", "fsdp"), scatter_dimension=0, tiled=True)
    return moe_out, token_grad, summed.reshape(1, -1, 3, hidden)


def solution(mesh):
    placed = P(ALL, None)
    weights = P("expert", ("dp", "fsdp"), None, None)
    sizes = mesh.shape
    steps = sizes["expert"] // 2
    small = sizes["dp"] == 2 and sizes["fsdp"] == 2 and steps > 1
    small = small and sizes["expert"] % 2 == 0 and steps & (steps - 1) == 0
    return jax.shard_map(
        paired if small else gathered,
        mesh=mesh,
        in_specs=(placed, placed, placed, weights, placed),
        out_specs=(placed, placed, weights),
        check_vma=False,
    )
```

```python
import jax
import jax.numpy as jnp
from jax import lax
from jax.sharding import PartitionSpec as P


CAP = 24
ALL = ("dp", "fsdp", "expert")
F32 = jnp.float32
BF16 = jnp.bfloat16


def route_tables(expert_ids, gate_units, slot_expert, slot_rank):
    tok_count, _ = expert_ids.shape
    same = expert_ids[:, :, None] == slot_expert[None, None, :]
    named = jnp.sum(same.astype(F32), axis=1)
    gates = jnp.sum(jnp.where(same, gate_units.astype(F32)[:, :, None], 0.0), axis=1)
    order = jnp.arange(tok_count, dtype=jnp.int32)
    earlier = (order[:, None] > order[None, :]).astype(BF16)
    before = jnp.dot(earlier, named.astype(BF16), preferred_element_type=F32)
    hit = (named > 0.5) & (before == slot_rank.astype(F32)[None, :])
    dispatch = hit.astype(BF16)
    combine = jnp.where(hit, gates / 256.0, 0.0).astype(BF16)
    return dispatch, combine


def contract(left, right, left_dim, right_dim):
    return lax.dot_general(
        left, right, (((left_dim,), (right_dim,)), ((), ())), preferred_element_type=F32
    )


class Moves:
    def __init__(self, dp, fsdp, experts):
        self.shape = (dp, fsdp, experts)

    def move(self, value, where):
        dp, fsdp, experts = self.shape
        pairs = []
        for d in range(dp):
            for f in range(fsdp):
                for e in range(experts):
                    nd, nf, ne = where(d, f, e)
                    pairs.append(((d * fsdp + f) * experts + e, (nd * fsdp + nf) * experts + ne))
        return lax.ppermute(value, ALL, pairs)

    def core(self, value):
        return self.move(value, lambda d, f, e: (d, f, e ^ 1))

    def weight_pair(self, value):
        return self.move(value, lambda d, f, e: (d, 1 - f, e) if e % 2 == 0 else (1 - d, f, e))

    def column_pair(self, value):
        return self.move(value, lambda d, f, e: (1 - d, f, e) if e % 2 == 0 else (d, 1 - f, e))

    def along_z(self, value, step):
        return self.move(value, lambda d, f, e: (d, f, e ^ (2 * step)))


def z_order(steps):
    return sorted(range(1, steps), key=lambda step: (step < 2, step))


def paired(tokens, expert_ids, gate_units, expert_weights, out_grad):
    return paired_body(tokens, expert_ids, gate_units, expert_weights, out_grad)


def paired_body(tokens, expert_ids, gate_units, expert_weights, out_grad):
    moves = Moves(*(lax.axis_size(name) for name in ALL))
    steps = moves.shape[2] // 2
    model_width = tokens.shape[1]
    quarter_width = model_width // 4
    half_width = model_width // 2
    hidden = expert_weights.shape[3]
    own_e = lax.axis_index("expert")
    own_z, own_c = own_e // 2, own_e % 2
    own_q = lax.axis_index("dp") * 2 + lax.axis_index("fsdp")
    quarter = (own_q, own_q ^ (1 + own_c), own_q ^ (2 - own_c), own_q ^ 3)
    half = steps * CAP

    weights_own = expert_weights[0]
    weights_far = moves.weight_pair(weights_own)
    pair = (weights_own, weights_far)

    slot = jnp.arange(2 * half, dtype=jnp.int32)
    slot_expert = ((slot % half // CAP) ^ own_z) * 2 + ((slot // half) ^ own_c)
    dispatch, combine = route_tables(expert_ids, gate_units, slot_expert, slot % CAP)

    def interleaved(first, second):
        width = first.shape[1]
        both = (first.reshape(steps, CAP, width), second.reshape(steps, CAP, width))
        return jnp.stack(both, axis=1).reshape(2 * half, width)

    def taken(array, *which):
        return jnp.concatenate(
            [
                lax.dynamic_slice_in_dim(array, quarter[i] * quarter_width, quarter_width, 1)
                for i in which
            ],
            axis=1,
        )

    def placed(own, out):
        whole = jnp.zeros((own.shape[0], model_width), BF16)
        for index in range(4):
            part = (own, out)[index // 2]
            low = index % 2 * quarter_width
            whole = lax.dynamic_update_slice_in_dim(
                whole, part[:, low : low + quarter_width], quarter[index] * quarter_width, 1
            )
        return whole

    def send_local(table, source):
        both = contract(table, source, 0, 0).astype(BF16)
        same = both[:half]
        came = moves.core(both[half:])
        own = interleaved(taken(same, 0, 1), taken(came, 0, 1))
        out = interleaved(taken(same, 2, 3), taken(came, 2, 3))
        return own, moves.column_pair(out)

    def by_z(rows):
        parts = [value.shape[0] // steps for value in rows]
        order = z_order(steps)
        pieces = []
        fenced = lax.optimization_barrier(tuple(rows))
        for step in order:
            piece = [v[step * n : (step + 1) * n] for v, n in zip(fenced, parts)]
            pieces.append(jnp.concatenate(piece) if len(piece) > 1 else piece[0])
        pieces = lax.optimization_barrier(tuple(pieces))
        got = {0: jnp.concatenate([v[:n] for v, n in zip(rows, parts)])}
        for step, piece in zip(order, pieces):
            got[step] = moves.along_z(piece, step)
        whole, low = [], 0
        for n in parts:
            whole.append(jnp.concatenate([got[i][low : low + n] for i in range(steps)]))
            low += n
        return whole

    def give_back_in(table, own, near):
        out = moves.column_pair(near)

        def source(array, index):
            return array.reshape(steps, 2, CAP, half_width)[:, index].reshape(half, half_width)

        came = moves.core(placed(source(own, 1), source(out, 1)))
        rows = jnp.concatenate([placed(source(own, 0), source(out, 0)), came])
        return contract(table, rows, 1, 0).astype(BF16)

    def inward(rows, which, sides=(0, 1)):
        return sum(
            contract(
                rows[:, i * quarter_width : (i + 1) * quarter_width], pair[i][:, which], 1, 0
            )
            for i in sides
        )

    def outward(terms):
        return jnp.concatenate(
            [
                sum(contract(value, pair[i][:, which], 1, 1) for value, which in terms)
                for i in (0, 1)
            ],
            axis=1,
        ).astype(BF16)

    def base(rows):
        return tuple(lax.optimization_barrier([inward(rows, i, (0,)) for i in (0, 1)]))

    def added(start, rows):
        both = [value + inward(rows, i, (1,)) for i, value in enumerate(start)]
        return jnp.concatenate(both, axis=1)

    rows_own, rows_near = send_local(dispatch, tokens)
    (rows_own,) = by_z([rows_own])
    (rows_near,) = by_z([rows_near])
    scaled_own, scaled_near = by_z(send_local(combine, out_grad))

    base_own = base(rows_own)
    base_near = base(rows_near)
    part_own = added(base_own, rows_own)
    message = part_own.astype(BF16)
    near_extra = moves.column_pair(message)
    part_near = added(base_near, rows_near)
    message = part_near.astype(BF16)
    own_extra = moves.column_pair(message)

    def act(part, extra):
        total = part + extra.astype(F32)
        gate_act, up_act = total[:, :hidden], total[:, hidden:]
        sigmoid_gate = jax.nn.sigmoid(gate_act)
        swish_gate = gate_act * sigmoid_gate
        slope = up_act * sigmoid_gate * (1.0 + gate_act * (1.0 - sigmoid_gate))
        return lax.optimization_barrier(((swish_gate * up_act).astype(BF16), slope, swish_gate))

    act_near, slope_near, swish_near = act(part_near, near_extra)
    out_near = outward([(act_near, 2)])
    act_own, slope_own, swish_own = act(part_own, own_extra)
    out_own = outward([(act_own, 2)])
    back_near, back_own = by_z([out_near, out_own])

    hid_own, hid_near = inward(scaled_own, 2), inward(scaled_near, 2)
    message = jnp.concatenate([hid_near, hid_own]).astype(BF16)
    extra = moves.column_pair(message)
    hid_own = hid_own + extra[: 2 * half].astype(F32)
    hid_near = hid_near + extra[2 * half :].astype(F32)
    gg_near, ug_near = (hid_near * slope_near).astype(BF16), (hid_near * swish_near).astype(BF16)
    gg_own, ug_own = (hid_own * slope_own).astype(BF16), (hid_own * swish_own).astype(BF16)

    rows = jnp.concatenate([rows_own, rows_near])
    scaled = jnp.concatenate([scaled_own, scaled_near])
    activation = jnp.concatenate([act_own, act_near])
    gate_grad = jnp.concatenate([gg_own, gg_near])
    up_grad = jnp.concatenate([ug_own, ug_near])
    first, second = slice(0, quarter_width), slice(quarter_width, half_width)
    term_far = contract(scaled[:, second], activation, 0, 0).astype(BF16)
    arrived_down = moves.weight_pair(term_far)
    grad_near = outward([(gg_near, 0), (ug_near, 1)])
    (grad_near,) = by_z([grad_near])
    terms_far = jnp.stack(
        [contract(rows[:, second], value, 0, 0) for value in (gate_grad, up_grad)]
    ).astype(BF16)
    arrived_in = moves.weight_pair(terms_far)
    grad_own = outward([(gg_own, 0), (ug_own, 1)])
    (grad_own,) = by_z([grad_own])
    moe_out = give_back_in(combine, back_own, back_near)
    token_grad = give_back_in(dispatch, grad_own, grad_near)
    term_down = contract(scaled[:, first], activation, 0, 0) + arrived_down.astype(F32)
    term_down = term_down.astype(BF16)
    terms = [
        contract(rows[:, first], value, 0, 0) + arrived_in[i].astype(F32)
        for i, value in enumerate((gate_grad, up_grad))
    ]
    weight_grad = jnp.stack([*(term.astype(BF16) for term in terms), term_down], axis=1)
    return moe_out, token_grad, weight_grad[None]


def gathered(tokens, expert_ids, gate_units, expert_weights, out_grad):
    experts = lax.axis_size("expert")
    slots = experts * CAP
    width = tokens.shape[1]
    hidden = expert_weights.shape[3]
    slot = jnp.arange(slots, dtype=jnp.int32)
    dispatch, combine = route_tables(expert_ids, gate_units, slot // CAP, slot % CAP)

    def exchange(rows):
        return lax.all_to_all(
            rows.reshape(experts, CAP, width), "expert", split_axis=0, concat_axis=0, tiled=True
        ).reshape(slots, width)

    slot_rows = exchange(contract(dispatch, tokens, 0, 0).astype(BF16))
    scaled = exchange(contract(combine, out_grad, 0, 0).astype(BF16))
    full = lax.all_gather(expert_weights, ("dp", "fsdp"), axis=1, tiled=True)[0]
    gate_act = contract(slot_rows, full[:, 0], 1, 0)
    up_act = contract(slot_rows, full[:, 1], 1, 0)
    sigmoid_gate = jax.nn.sigmoid(gate_act)
    swish_gate = gate_act * sigmoid_gate
    activation = (swish_gate * up_act).astype(BF16)
    result = contract(activation, full[:, 2], 1, 1).astype(BF16)
    moe_out = contract(combine, exchange(result), 1, 0).astype(BF16)
    hidden_grad = contract(scaled, full[:, 2], 1, 0)
    gate_grad = (
        hidden_grad * up_act * sigmoid_gate * (1.0 + gate_act * (1.0 - sigmoid_gate))
    ).astype(BF16)
    up_grad = (hidden_grad * swish_gate).astype(BF16)
    row_grad = (
        contract(gate_grad, full[:, 0], 1, 1) + contract(up_grad, full[:, 1], 1, 1)
    ).astype(BF16)
    token_grad = contract(dispatch, exchange(row_grad), 1, 0).astype(BF16)
    term = jnp.stack(
        [
            contract(slot_rows, gate_grad, 0, 0),
            contract(slot_rows, up_grad, 0, 0),
            contract(scaled, activation, 0, 0),
        ],
        axis=1,
    ).astype(BF16)
    summed = lax.psum_scatter(term, ("dp", "fsdp"), scatter_dimension=0, tiled=True)
    return moe_out, token_grad, summed.reshape(1, -1, 3, hidden)


def solution(mesh):
    placed = P(ALL, None)
    weights = P("expert", ("dp", "fsdp"), None, None)
    sizes = mesh.shape
    steps = sizes["expert"] // 2
    small = sizes["dp"] == 2 and sizes["fsdp"] == 2 and steps > 1
    small = small and sizes["expert"] % 2 == 0 and steps & (steps - 1) == 0
    return jax.shard_map(
        paired if small else gathered,
        mesh=mesh,
        in_specs=(placed, placed, placed, weights, placed),
        out_specs=(placed, placed, weights),
        check_vma=False,
    )
```

```python
import jax
import jax.numpy as jnp
from jax import lax
from jax.experimental import pallas as pl
from jax.experimental.pallas import tpu as pltpu
from jax.sharding import PartitionSpec as P


CAP = 24
ALL = ("dp", "fsdp", "expert")
F32 = jnp.float32
BF16 = jnp.bfloat16


def route_tables(expert_ids, gate_units, slot_expert, slot_rank):
    tok_count, _ = expert_ids.shape
    same = expert_ids[:, :, None] == slot_expert[None, None, :]
    named = jnp.sum(same.astype(F32), axis=1)
    gates = jnp.sum(jnp.where(same, gate_units.astype(F32)[:, :, None], 0.0), axis=1)
    order = jnp.arange(tok_count, dtype=jnp.int32)
    earlier = (order[:, None] > order[None, :]).astype(BF16)
    before = jnp.dot(earlier, named.astype(BF16), preferred_element_type=F32)
    hit = (named > 0.5) & (before == slot_rank.astype(F32)[None, :])
    dispatch = hit.astype(BF16)
    combine = jnp.where(hit, gates / 256.0, 0.0).astype(BF16)
    return dispatch, combine


def contract(left, right, left_dim, right_dim):
    return lax.dot_general(
        left, right, (((left_dim,), (right_dim,)), ((), ())), preferred_element_type=F32
    )


VMEM = pl.BlockSpec(memory_space=pltpu.VMEM)
HBM = pl.BlockSpec(memory_space=pltpu.HBM)
PARAMS = pltpu.CompilerParams(vmem_limit_bytes=8 << 20)


def where_am_i():
    own_e = lax.axis_index("expert")
    own_c = lax.rem(own_e, 2)
    own_q = lax.axis_index("dp") * 2 + lax.axis_index("fsdp")
    quarter = (
        own_q,
        jnp.bitwise_xor(own_q, 1 + own_c),
        jnp.bitwise_xor(own_q, 2 - own_c),
        jnp.bitwise_xor(own_q, 3),
    )
    return lax.div(own_e, 2), own_c, quarter


def quarter_at(quarter, index, width):
    return pl.ds(pl.multiple_of(quarter[index] * width, width), width)


def write_rows(table, held, own, out, other):
    half, width = own.shape[0], held.shape[1] // 4
    _, _, quarter = where_am_i()
    for index in range(4):
        rows = jnp.dot(
            table, held[:, quarter_at(quarter, index, width)], preferred_element_type=F32
        ).astype(BF16)
        low = index % 2 * width
        (own, out)[index // 2][:, low : low + width] = rows[:half]
        low = (0, 2, 1, 3)[index] * width
        other[:, low : low + width] = rows[half:]


def row_shapes(half, width):
    return [
        jax.ShapeDtypeStruct((half, width // 2), BF16),
        jax.ShapeDtypeStruct((half, width // 2), BF16),
        jax.ShapeDtypeStruct((half, width), BF16),
    ]


def front(ids, gates, source, steps):
    top_count, tok_count = ids.shape
    half, slots = steps * CAP, 2 * steps * CAP

    def kernel(ids_hbm, gates_hbm, source_hbm, own, out, other, dispatch, combine, *scratch):
        ids_ref, gates_ref, held, sem = scratch
        fetches = [
            pltpu.make_async_copy(ids_hbm, ids_ref, sem.at[0]),
            pltpu.make_async_copy(gates_hbm, gates_ref, sem.at[1]),
            pltpu.make_async_copy(source_hbm, held, sem.at[2]),
        ]
        for fetch in fetches:
            fetch.start()
        own_z, own_c, _ = where_am_i()
        slot = lax.broadcasted_iota(jnp.int32, (slots, 1), 0)
        expert, rank = jnp.zeros_like(slot), slot
        for block in range(2 * steps):
            inside = (slot >= block * CAP) & (slot < (block + 1) * CAP)
            number = jnp.bitwise_xor(block % steps, own_z) * 2
            number = number + jnp.bitwise_xor(block // steps, own_c)
            expert = jnp.where(inside, number, expert)
            rank = jnp.where(inside, slot - block * CAP, rank)
        row = lax.broadcasted_iota(jnp.int32, (tok_count, tok_count), 0)
        col = lax.broadcasted_iota(jnp.int32, (tok_count, tok_count), 1)
        earlier = jnp.where(row < col, 1.0, 0.0).astype(BF16)
        named = jnp.zeros((slots, tok_count), F32)
        value = jnp.zeros((slots, tok_count), F32)
        fetches[0].wait()
        fetches[1].wait()
        for k in range(top_count):
            hit = ids_ref[k : k + 1, :] == expert
            named = jnp.where(hit, 1.0, named)
            value = jnp.where(hit, gates_ref[k : k + 1, :].astype(F32), value)
        before = jnp.dot(named.astype(BF16), earlier, preferred_element_type=F32)
        chosen = (named > 0.5) & (before == rank.astype(F32))
        table = jnp.where(chosen, 1.0, 0.0).astype(BF16)
        dispatch[...] = table
        combine[...] = jnp.where(chosen, value * (1.0 / 256.0), 0.0).astype(BF16)
        fetches[2].wait()
        write_rows(table, held, own, out, other)

    tables = [jax.ShapeDtypeStruct((slots, tok_count), BF16)] * 2
    return pl.pallas_call(
        kernel,
        out_shape=(*row_shapes(half, source.shape[1]), *tables),
        in_specs=[HBM] * 3,
        out_specs=(VMEM,) * 5,
        scratch_shapes=[
            pltpu.VMEM(ids.shape, jnp.int32),
            pltpu.VMEM(gates.shape, jnp.int32),
            pltpu.VMEM(source.shape, BF16),
            pltpu.SemaphoreType.DMA((3,)),
        ],
        compiler_params=PARAMS,
        name="front",
    )(ids, gates, source)


def local_rows(table, source):
    def kernel(table_ref, source_ref, own, out, other):
        write_rows(table_ref[...], source_ref, own, out, other)

    return pl.pallas_call(
        kernel,
        out_shape=row_shapes(table.shape[0] // 2, source.shape[1]),
        in_specs=[VMEM] * 2,
        out_specs=(VMEM,) * 3,
        compiler_params=PARAMS,
        name="local_rows",
    )(table, source)


def split_weights(weights):
    parts, depth, hidden = weights.shape

    def kernel(source, gates, down, sem):
        copies = [
            pltpu.make_async_copy(source.at[pl.ds(0, parts - 1)], gates, sem.at[0]),
            pltpu.make_async_copy(source.at[parts - 1], down, sem.at[1]),
        ]
        for copy in copies:
            copy.start()
        for copy in copies:
            copy.wait()

    return pl.pallas_call(
        kernel,
        out_shape=(
            jax.ShapeDtypeStruct((parts - 1, depth, hidden), weights.dtype),
            jax.ShapeDtypeStruct((depth, hidden), weights.dtype),
        ),
        in_specs=[HBM],
        out_specs=(VMEM,) * 2,
        scratch_shapes=[pltpu.SemaphoreType.DMA((2,))],
        compiler_params=PARAMS,
        name="split_weights",
    )(weights)


def weight_terms(rows, grads, arrived, down):
    parts, depth, hidden = arrived.shape

    def kernel(rows_ref, gate_ref, up_ref, arrived_ref, down_ref, answer, held, sem):
        writes = [pltpu.make_async_copy(down_ref, answer.at[parts], sem.at[parts])]
        writes[0].start()
        for part, grad in enumerate((gate_ref, up_ref)):
            term = contract(rows_ref[:, :depth], grad[...], 0, 0)
            held[part] = (term + arrived_ref[part].astype(F32)).astype(BF16)
            writes.append(pltpu.make_async_copy(held.at[part], answer.at[part], sem.at[part]))
            writes[-1].start()
        for write in writes:
            write.wait()

    return pl.pallas_call(
        kernel,
        out_shape=jax.ShapeDtypeStruct((parts + 1, depth, hidden), BF16),
        in_specs=[VMEM] * 5,
        out_specs=HBM,
        scratch_shapes=[
            pltpu.VMEM(arrived.shape, BF16),
            pltpu.SemaphoreType.DMA((parts + 1,)),
        ],
        compiler_params=PARAMS,
        name="weight_terms",
    )(rows, *grads, arrived, down)


def fold(table, own, out, came):
    tok_count, width = table.shape[1], came.shape[1] // 4

    def kernel(table_ref, own_ref, out_ref, came_ref, answer, held, sem):
        _, _, quarter = where_am_i()
        writes = []
        for index in range(4):
            low = index % 2 * width
            first = (own_ref, out_ref)[index // 2][:, low : low + width]
            rows = jnp.concatenate([first, came_ref[:, index * width : (index + 1) * width]])
            held[index] = contract(table_ref[...], rows, 0, 0).astype(BF16)
            writes.append(
                pltpu.make_async_copy(
                    held.at[index],
                    answer.at[:, quarter_at(quarter, index, width)],
                    sem.at[index],
                )
            )
            writes[-1].start()
        for write in writes:
            write.wait()

    return pl.pallas_call(
        kernel,
        out_shape=jax.ShapeDtypeStruct((tok_count, came.shape[1]), BF16),
        in_specs=[VMEM] * 4,
        out_specs=HBM,
        scratch_shapes=[pltpu.VMEM((4, tok_count, width), BF16), pltpu.SemaphoreType.DMA((4,))],
        compiler_params=PARAMS,
        name="fold",
    )(table, own, out, came)


class Moves:
    def __init__(self, dp, fsdp, experts):
        self.shape = (dp, fsdp, experts)

    def move(self, value, where):
        dp, fsdp, experts = self.shape
        pairs = []
        for d in range(dp):
            for f in range(fsdp):
                for e in range(experts):
                    nd, nf, ne = where(d, f, e)
                    pairs.append(((d * fsdp + f) * experts + e, (nd * fsdp + nf) * experts + ne))
        return lax.ppermute(value, ALL, pairs)

    def core(self, value):
        return self.move(value, lambda d, f, e: (d, f, e ^ 1))

    def weight_pair(self, value):
        return self.move(value, lambda d, f, e: (d, 1 - f, e) if e % 2 == 0 else (1 - d, f, e))

    def column_pair(self, value):
        return self.move(value, lambda d, f, e: (1 - d, f, e) if e % 2 == 0 else (d, 1 - f, e))

    def along_z(self, value, step):
        return self.move(value, lambda d, f, e: (d, f, e ^ (2 * step)))


def z_order(steps):
    return sorted(range(1, steps), key=lambda step: (step < 2, step))


def paired(tokens, expert_ids, gate_units, expert_weights, out_grad):
    return paired_body(tokens, expert_ids, gate_units, expert_weights, out_grad)


def paired_body(tokens, expert_ids, gate_units, expert_weights, out_grad):
    moves = Moves(*(lax.axis_size(name) for name in ALL))
    steps = moves.shape[2] // 2
    model_width = tokens.shape[1]
    quarter_width = model_width // 4
    half_width = model_width // 2
    hidden = expert_weights.shape[3]
    half = steps * CAP

    gates_own, down_own = split_weights(jnp.transpose(expert_weights[0], (1, 0, 2)))
    gates_far = moves.weight_pair(gates_own)
    pair = (
        (gates_own[0], gates_own[1], down_own),
        (gates_far[0], gates_far[1], moves.weight_pair(down_own)),
    )

    *token_parts, dispatch, combine = front(expert_ids.T, gate_units.T, tokens, steps)

    def interleaved(first, second):
        width = first.shape[1]
        both = (first.reshape(steps, CAP, width), second.reshape(steps, CAP, width))
        return jnp.stack(both, axis=1).reshape(2 * half, width)

    def send_local(own, out, other):
        came = moves.core(other)
        own = interleaved(own, came[:, :half_width])
        out = interleaved(out, came[:, half_width:])
        return own, moves.column_pair(out)

    def by_z(rows):
        parts = [value.shape[0] // steps for value in rows]
        order = z_order(steps)
        pieces = []
        fenced = lax.optimization_barrier(tuple(rows))
        for step in order:
            piece = [v[step * n : (step + 1) * n] for v, n in zip(fenced, parts)]
            pieces.append(jnp.concatenate(piece) if len(piece) > 1 else piece[0])
        pieces = lax.optimization_barrier(tuple(pieces))
        got = {0: jnp.concatenate([v[:n] for v, n in zip(rows, parts)])}
        for step, piece in zip(order, pieces):
            got[step] = moves.along_z(piece, step)
        whole, low = [], 0
        for n in parts:
            whole.append(jnp.concatenate([got[i][low : low + n] for i in range(steps)]))
            low += n
        return whole

    def give_back_in(table, own, near):
        out = moves.column_pair(near)

        def source(array, index):
            return array.reshape(steps, 2, CAP, half_width)[:, index].reshape(half, half_width)

        parts = [
            side[:, i * quarter_width : (i + 1) * quarter_width]
            for i in (0, 1)
            for side in (source(own, 1), source(out, 1))
        ]
        came = moves.core(jnp.concatenate(parts, axis=1))
        return fold(table, source(own, 0), source(out, 0), came)

    def inward(rows, which, sides=(0, 1)):
        return sum(
            contract(
                rows[:, i * quarter_width : (i + 1) * quarter_width], pair[i][which], 1, 0
            )
            for i in sides
        )

    def outward(terms):
        return jnp.concatenate(
            [
                sum(contract(value, pair[i][which], 1, 1) for value, which in terms)
                for i in (0, 1)
            ],
            axis=1,
        ).astype(BF16)

    def base(rows):
        return tuple(lax.optimization_barrier([inward(rows, i, (0,)) for i in (0, 1)]))

    def added(start, rows):
        both = [value + inward(rows, i, (1,)) for i, value in enumerate(start)]
        return jnp.concatenate(both, axis=1)

    rows_own, rows_near = send_local(*token_parts)
    (rows_own,) = by_z([rows_own])
    (rows_near,) = by_z([rows_near])
    grad_parts = local_rows(combine, out_grad)
    scaled_own, scaled_near = by_z(send_local(*grad_parts))

    base_own = base(rows_own)
    base_near = base(rows_near)
    part_own = added(base_own, rows_own)
    message = part_own.astype(BF16)
    near_extra = moves.column_pair(message)
    part_near = added(base_near, rows_near)
    message = part_near.astype(BF16)
    own_extra = moves.column_pair(message)

    def act(part, extra):
        total = part + extra.astype(F32)
        gate_act, up_act = total[:, :hidden], total[:, hidden:]
        sigmoid_gate = jax.nn.sigmoid(gate_act)
        swish_gate = gate_act * sigmoid_gate
        slope = up_act * sigmoid_gate * (1.0 + gate_act * (1.0 - sigmoid_gate))
        return lax.optimization_barrier(((swish_gate * up_act).astype(BF16), slope, swish_gate))

    act_near, slope_near, swish_near = act(part_near, near_extra)
    out_near = outward([(act_near, 2)])
    act_own, slope_own, swish_own = act(part_own, own_extra)
    out_own = outward([(act_own, 2)])
    (back_near,) = by_z([out_near])
    (back_own,) = by_z([out_own])

    hid_own, hid_near = inward(scaled_own, 2), inward(scaled_near, 2)
    message = jnp.concatenate([hid_near, hid_own]).astype(BF16)
    extra = moves.column_pair(message)
    hid_own = hid_own + extra[: 2 * half].astype(F32)
    hid_near = hid_near + extra[2 * half :].astype(F32)
    gg_near, ug_near = (hid_near * slope_near).astype(BF16), (hid_near * swish_near).astype(BF16)
    gg_own, ug_own = (hid_own * slope_own).astype(BF16), (hid_own * swish_own).astype(BF16)

    rows = jnp.concatenate([rows_own, rows_near])
    scaled = jnp.concatenate([scaled_own, scaled_near])
    activation = jnp.concatenate([act_own, act_near])
    gate_grad = jnp.concatenate([gg_own, gg_near])
    up_grad = jnp.concatenate([ug_own, ug_near])
    first, second = slice(0, quarter_width), slice(quarter_width, half_width)
    term_far = contract(scaled[:, second], activation, 0, 0).astype(BF16)
    arrived_down = moves.weight_pair(term_far)
    grad_near = outward([(gg_near, 0), (ug_near, 1)])
    (grad_near,) = by_z([grad_near])
    terms_far = jnp.stack(
        [contract(rows[:, second], value, 0, 0) for value in (gate_grad, up_grad)]
    ).astype(BF16)
    arrived_in = moves.weight_pair(terms_far)
    grad_own = outward([(gg_own, 0), (ug_own, 1)])
    (grad_own,) = by_z([grad_own])
    moe_out = give_back_in(combine, back_own, back_near)
    token_grad = give_back_in(dispatch, grad_own, grad_near)
    term_down = contract(scaled[:, first], activation, 0, 0) + arrived_down.astype(F32)
    term_down = term_down.astype(BF16)
    weight_grad = weight_terms(rows, (gate_grad, up_grad), arrived_in, term_down)
    return moe_out, token_grad, jnp.transpose(weight_grad, (1, 0, 2))[None]


def gathered(tokens, expert_ids, gate_units, expert_weights, out_grad):
    experts = lax.axis_size("expert")
    slots = experts * CAP
    width = tokens.shape[1]
    hidden = expert_weights.shape[3]
    slot = jnp.arange(slots, dtype=jnp.int32)
    dispatch, combine = route_tables(expert_ids, gate_units, slot // CAP, slot % CAP)

    def exchange(rows):
        return lax.all_to_all(
            rows.reshape(experts, CAP, width), "expert", split_axis=0, concat_axis=0, tiled=True
        ).reshape(slots, width)

    slot_rows = exchange(contract(dispatch, tokens, 0, 0).astype(BF16))
    scaled = exchange(contract(combine, out_grad, 0, 0).astype(BF16))
    full = lax.all_gather(expert_weights, ("dp", "fsdp"), axis=1, tiled=True)[0]
    gate_act = contract(slot_rows, full[:, 0], 1, 0)
    up_act = contract(slot_rows, full[:, 1], 1, 0)
    sigmoid_gate = jax.nn.sigmoid(gate_act)
    swish_gate = gate_act * sigmoid_gate
    activation = (swish_gate * up_act).astype(BF16)
    result = contract(activation, full[:, 2], 1, 1).astype(BF16)
    moe_out = contract(combine, exchange(result), 1, 0).astype(BF16)
    hidden_grad = contract(scaled, full[:, 2], 1, 0)
    gate_grad = (
        hidden_grad * up_act * sigmoid_gate * (1.0 + gate_act * (1.0 - sigmoid_gate))
    ).astype(BF16)
    up_grad = (hidden_grad * swish_gate).astype(BF16)
    row_grad = (
        contract(gate_grad, full[:, 0], 1, 1) + contract(up_grad, full[:, 1], 1, 1)
    ).astype(BF16)
    token_grad = contract(dispatch, exchange(row_grad), 1, 0).astype(BF16)
    term = jnp.stack(
        [
            contract(slot_rows, gate_grad, 0, 0),
            contract(slot_rows, up_grad, 0, 0),
            contract(scaled, activation, 0, 0),
        ],
        axis=1,
    ).astype(BF16)
    summed = lax.psum_scatter(term, ("dp", "fsdp"), scatter_dimension=0, tiled=True)
    return moe_out, token_grad, summed.reshape(1, -1, 3, hidden)


def solution(mesh):
    placed = P(ALL, None)
    weights = P("expert", ("dp", "fsdp"), None, None)
    sizes = mesh.shape
    steps = sizes["expert"] // 2
    small = sizes["dp"] == 2 and sizes["fsdp"] == 2 and steps > 1
    small = small and sizes["expert"] % 2 == 0 and steps & (steps - 1) == 0
    return jax.shard_map(
        paired if small else gathered,
        mesh=mesh,
        in_specs=(placed, placed, placed, weights, placed),
        out_specs=(placed, placed, weights),
        check_vma=False,
    )
```

```python
import jax
import jax.numpy as jnp
from jax import lax
from jax.experimental import pallas as pl
from jax.experimental.pallas import tpu as pltpu
from jax.sharding import PartitionSpec as P


CAP = 24
ALL = ("dp", "fsdp", "expert")
F32 = jnp.float32
BF16 = jnp.bfloat16


def route_tables(expert_ids, gate_units, slot_expert, slot_rank):
    tok_count, _ = expert_ids.shape
    same = expert_ids[:, :, None] == slot_expert[None, None, :]
    named = jnp.sum(same.astype(F32), axis=1)
    gates = jnp.sum(jnp.where(same, gate_units.astype(F32)[:, :, None], 0.0), axis=1)
    order = jnp.arange(tok_count, dtype=jnp.int32)
    earlier = (order[:, None] > order[None, :]).astype(BF16)
    before = jnp.dot(earlier, named.astype(BF16), preferred_element_type=F32)
    hit = (named > 0.5) & (before == slot_rank.astype(F32)[None, :])
    dispatch = hit.astype(BF16)
    combine = jnp.where(hit, gates / 256.0, 0.0).astype(BF16)
    return dispatch, combine


def contract(left, right, left_dim, right_dim):
    return lax.dot_general(
        left, right, (((left_dim,), (right_dim,)), ((), ())), preferred_element_type=F32
    )


VMEM = pl.BlockSpec(memory_space=pltpu.VMEM)
HBM = pl.BlockSpec(memory_space=pltpu.HBM)
PARAMS = pltpu.CompilerParams(vmem_limit_bytes=8 << 20)


def where_am_i():
    own_e = lax.axis_index("expert")
    own_c = lax.rem(own_e, 2)
    own_q = lax.axis_index("dp") * 2 + lax.axis_index("fsdp")
    quarter = (
        own_q,
        jnp.bitwise_xor(own_q, 1 + own_c),
        jnp.bitwise_xor(own_q, 2 - own_c),
        jnp.bitwise_xor(own_q, 3),
    )
    return lax.div(own_e, 2), own_c, quarter


def quarter_at(quarter, index, width):
    return pl.ds(pl.multiple_of(quarter[index] * width, width), width)


def write_rows(table, held, own, out, other):
    half, width = own.shape[0], held.shape[1] // 4
    _, _, quarter = where_am_i()
    for index in range(4):
        rows = jnp.dot(
            table, held[:, quarter_at(quarter, index, width)], preferred_element_type=F32
        ).astype(BF16)
        low = index % 2 * width
        (own, out)[index // 2][:, low : low + width] = rows[:half]
        low = (0, 2, 1, 3)[index] * width
        other[:, low : low + width] = rows[half:]


def row_shapes(half, width):
    return [
        jax.ShapeDtypeStruct((half, width // 2), BF16),
        jax.ShapeDtypeStruct((half, width // 2), BF16),
        jax.ShapeDtypeStruct((half, width), BF16),
    ]


def front(ids, gates, source, steps):
    top_count, tok_count = ids.shape
    half, slots = steps * CAP, 2 * steps * CAP

    def kernel(ids_hbm, gates_hbm, source_hbm, own, out, other, dispatch, combine, *scratch):
        ids_ref, gates_ref, held, sem = scratch
        fetches = [
            pltpu.make_async_copy(ids_hbm, ids_ref, sem.at[0]),
            pltpu.make_async_copy(gates_hbm, gates_ref, sem.at[1]),
            pltpu.make_async_copy(source_hbm, held, sem.at[2]),
        ]
        for fetch in fetches:
            fetch.start()
        own_z, own_c, _ = where_am_i()
        slot = lax.broadcasted_iota(jnp.int32, (slots, 1), 0)
        expert, rank = jnp.zeros_like(slot), slot
        for block in range(2 * steps):
            inside = (slot >= block * CAP) & (slot < (block + 1) * CAP)
            number = jnp.bitwise_xor(block % steps, own_z) * 2
            number = number + jnp.bitwise_xor(block // steps, own_c)
            expert = jnp.where(inside, number, expert)
            rank = jnp.where(inside, slot - block * CAP, rank)
        row = lax.broadcasted_iota(jnp.int32, (tok_count, tok_count), 0)
        col = lax.broadcasted_iota(jnp.int32, (tok_count, tok_count), 1)
        earlier = jnp.where(row < col, 1.0, 0.0).astype(BF16)
        named = jnp.zeros((slots, tok_count), F32)
        value = jnp.zeros((slots, tok_count), F32)
        fetches[0].wait()
        fetches[1].wait()
        for k in range(top_count):
            hit = ids_ref[k : k + 1, :] == expert
            named = jnp.where(hit, 1.0, named)
            value = jnp.where(hit, gates_ref[k : k + 1, :].astype(F32), value)
        before = jnp.dot(named.astype(BF16), earlier, preferred_element_type=F32)
        chosen = (named > 0.5) & (before == rank.astype(F32))
        table = jnp.where(chosen, 1.0, 0.0).astype(BF16)
        dispatch[...] = table
        combine[...] = jnp.where(chosen, value * (1.0 / 256.0), 0.0).astype(BF16)
        fetches[2].wait()
        write_rows(table, held, own, out, other)

    tables = [jax.ShapeDtypeStruct((slots, tok_count), BF16)] * 2
    return pl.pallas_call(
        kernel,
        out_shape=(*row_shapes(half, source.shape[1]), *tables),
        in_specs=[HBM] * 3,
        out_specs=(VMEM,) * 5,
        scratch_shapes=[
            pltpu.VMEM(ids.shape, jnp.int32),
            pltpu.VMEM(gates.shape, jnp.int32),
            pltpu.VMEM(source.shape, BF16),
            pltpu.SemaphoreType.DMA((3,)),
        ],
        compiler_params=PARAMS,
        name="front",
    )(ids, gates, source)


def local_rows(table, source):
    def kernel(table_ref, source_ref, own, out, other):
        write_rows(table_ref[...], source_ref, own, out, other)

    return pl.pallas_call(
        kernel,
        out_shape=row_shapes(table.shape[0] // 2, source.shape[1]),
        in_specs=[VMEM] * 2,
        out_specs=(VMEM,) * 3,
        compiler_params=PARAMS,
        name="local_rows",
    )(table, source)


def split_weights(weights):
    parts, depth, hidden = weights.shape

    def kernel(source, gates, down, sem):
        copies = [
            pltpu.make_async_copy(source.at[pl.ds(0, parts - 1)], gates, sem.at[0]),
            pltpu.make_async_copy(source.at[parts - 1], down, sem.at[1]),
        ]
        for copy in copies:
            copy.start()
        for copy in copies:
            copy.wait()

    return pl.pallas_call(
        kernel,
        out_shape=(
            jax.ShapeDtypeStruct((parts - 1, depth, hidden), weights.dtype),
            jax.ShapeDtypeStruct((depth, hidden), weights.dtype),
        ),
        in_specs=[HBM],
        out_specs=(VMEM,) * 2,
        scratch_shapes=[pltpu.SemaphoreType.DMA((2,))],
        compiler_params=PARAMS,
        name="split_weights",
    )(weights)


def first_terms(own, arrived, down):
    depth, hidden = own.shape

    def kernel(own_ref, arrived_ref, down_ref, answer, held, sem):
        copies = [pltpu.make_async_copy(down_ref, answer.at[2], sem.at[0])]
        copies[0].start()
        held[...] = (own_ref[...] + arrived_ref[...].astype(F32)).astype(BF16)
        copies.append(pltpu.make_async_copy(held, answer.at[0], sem.at[1]))
        copies[1].start()
        for copy in copies:
            copy.wait()

    return pl.pallas_call(
        kernel,
        out_shape=jax.ShapeDtypeStruct((3, depth, hidden), BF16),
        in_specs=[VMEM] * 3,
        out_specs=HBM,
        scratch_shapes=[pltpu.VMEM((depth, hidden), BF16), pltpu.SemaphoreType.DMA((2,))],
        compiler_params=PARAMS,
        name="first_terms",
    )(own, arrived, down)


def last_term(whole, own, arrived):
    depth, hidden = own.shape
    pieces = 4
    rows = depth // pieces

    def kernel(whole_ref, own_ref, arrived_ref, answer, held, sem):
        copies = []
        for i in range(pieces):
            span = pl.ds(i * rows, rows)
            held[span] = (own_ref[span, :] + arrived_ref[span, :].astype(F32)).astype(BF16)
            copies.append(pltpu.make_async_copy(held.at[span], answer.at[1, span], sem.at[i]))
            copies[i].start()
        for copy in copies:
            copy.wait()

    return pl.pallas_call(
        kernel,
        out_shape=jax.ShapeDtypeStruct(whole.shape, BF16),
        in_specs=[HBM, VMEM, VMEM],
        out_specs=HBM,
        scratch_shapes=[pltpu.VMEM((depth, hidden), BF16), pltpu.SemaphoreType.DMA((pieces,))],
        input_output_aliases={0: 0},
        compiler_params=PARAMS,
        name="last_term",
    )(whole, own, arrived)


def fold(table, same, other):
    tok_count, width = table.shape[1], same[0][0].shape[1] // 2
    arrays = list({id(array): array for array, _ in (*same, *other)}.values())
    number = {id(array): i for i, array in enumerate(arrays)}
    spots = [[(number[id(array)], block) for array, block in side] for side in (same, other)]

    def kernel(table_ref, *refs):
        sources, (answer, held, sem) = refs[: len(arrays)], refs[len(arrays) :]
        _, _, quarter = where_am_i()
        writes = []
        for index in range(4):
            parts = [side[index] for side in spots]
            rows = jnp.concatenate(
                [sources[i][:, block * width : (block + 1) * width] for i, block in parts]
            )
            held[index] = contract(table_ref[...], rows, 0, 0).astype(BF16)
            writes.append(
                pltpu.make_async_copy(
                    held.at[index],
                    answer.at[:, quarter_at(quarter, index, width)],
                    sem.at[index],
                )
            )
            writes[-1].start()
        for write in writes:
            write.wait()

    return pl.pallas_call(
        kernel,
        out_shape=jax.ShapeDtypeStruct((tok_count, 4 * width), BF16),
        in_specs=[VMEM] * (1 + len(arrays)),
        out_specs=HBM,
        scratch_shapes=[pltpu.VMEM((4, tok_count, width), BF16), pltpu.SemaphoreType.DMA((4,))],
        compiler_params=PARAMS,
        name="fold",
    )(table, *arrays)


class Moves:
    def __init__(self, dp, fsdp, experts):
        self.shape = (dp, fsdp, experts)

    def move(self, value, where):
        dp, fsdp, experts = self.shape
        pairs = []
        for d in range(dp):
            for f in range(fsdp):
                for e in range(experts):
                    nd, nf, ne = where(d, f, e)
                    pairs.append(((d * fsdp + f) * experts + e, (nd * fsdp + nf) * experts + ne))
        return lax.ppermute(value, ALL, pairs)

    def core(self, value):
        return self.move(value, lambda d, f, e: (d, f, e ^ 1))

    def weight_pair(self, value):
        return self.move(value, lambda d, f, e: (d, 1 - f, e) if e % 2 == 0 else (1 - d, f, e))

    def column_pair(self, value):
        return self.move(value, lambda d, f, e: (1 - d, f, e) if e % 2 == 0 else (d, 1 - f, e))

    def cross_pair(self, value):
        return self.move(
            value, lambda d, f, e: (1 - d, f, e ^ 1) if e % 2 == 0 else (d, 1 - f, e ^ 1)
        )

    def along_z(self, value, step):
        return self.move(value, lambda d, f, e: (d, f, e ^ (2 * step)))


def z_order(steps):
    return sorted(range(1, steps), key=lambda step: (step < 2, step))


def paired(tokens, expert_ids, gate_units, expert_weights, out_grad):
    return paired_body(tokens, expert_ids, gate_units, expert_weights, out_grad)


def paired_body(tokens, expert_ids, gate_units, expert_weights, out_grad):
    moves = Moves(*(lax.axis_size(name) for name in ALL))
    steps = moves.shape[2] // 2
    model_width = tokens.shape[1]
    quarter_width = model_width // 4
    half_width = model_width // 2
    hidden = expert_weights.shape[3]
    half = steps * CAP

    gates_own, down_own = split_weights(jnp.transpose(expert_weights[0], (1, 0, 2)))
    gates_far = moves.weight_pair(gates_own)
    pair = (
        (gates_own[0], gates_own[1], down_own),
        (gates_far[0], gates_far[1], moves.weight_pair(down_own)),
    )

    *token_parts, dispatch, combine = front(expert_ids.T, gate_units.T, tokens, steps)

    def interleaved(first, second):
        width = first.shape[1]
        both = (first.reshape(steps, CAP, width), second.reshape(steps, CAP, width))
        return jnp.stack(both, axis=1).reshape(2 * half, width)

    def send_local(own, out, other):
        came = moves.core(other)
        own = interleaved(own, came[:, :half_width])
        out = interleaved(out, came[:, half_width:])
        return own, moves.column_pair(out)

    def by_z(rows):
        parts = [value.shape[0] // steps for value in rows]
        order = z_order(steps)
        pieces = []
        fenced = lax.optimization_barrier(tuple(rows))
        for step in order:
            piece = [v[step * n : (step + 1) * n] for v, n in zip(fenced, parts)]
            pieces.append(jnp.concatenate(piece) if len(piece) > 1 else piece[0])
        pieces = lax.optimization_barrier(tuple(pieces))
        got = {0: jnp.concatenate([v[:n] for v, n in zip(rows, parts)])}
        for step, piece in zip(order, pieces):
            got[step] = moves.along_z(piece, step)
        whole, low = [], 0
        for n in parts:
            whole.append(jnp.concatenate([got[i][low : low + n] for i in range(steps)]))
            low += n
        return whole

    def source(array, index):
        return array.reshape(steps, 2, CAP, half_width)[:, index].reshape(half, half_width)

    def give_back(table, own, near):
        out = moves.column_pair(near)
        parts = [
            side[:, i * quarter_width : (i + 1) * quarter_width]
            for i in (0, 1)
            for side in (source(own, 1), source(out, 1))
        ]
        came = moves.core(jnp.concatenate(parts, axis=1))
        own, out = source(own, 0), source(out, 0)
        other = [(came, i) for i in range(4)]
        return fold(table, [(own, 0), (own, 1), (out, 0), (out, 1)], other)

    def give_back_crossed(table, own, near):
        out = moves.column_pair(source(near, 0))
        cross = moves.cross_pair(source(near, 1))
        came = moves.core(source(own, 1))
        own = source(own, 0)
        same = [(own, 0), (own, 1), (out, 0), (out, 1)]
        return fold(table, same, [(came, 0), (cross, 0), (came, 1), (cross, 1)])

    def inward(rows, which, sides=(0, 1)):
        return sum(
            contract(
                rows[:, i * quarter_width : (i + 1) * quarter_width], pair[i][which], 1, 0
            )
            for i in sides
        )

    def outward(terms):
        return jnp.concatenate(
            [
                sum(contract(value, pair[i][which], 1, 1) for value, which in terms)
                for i in (0, 1)
            ],
            axis=1,
        ).astype(BF16)

    def base(rows):
        return tuple(lax.optimization_barrier([inward(rows, i, (0,)) for i in (0, 1)]))

    def added(start, rows):
        both = [value + inward(rows, i, (1,)) for i, value in enumerate(start)]
        return jnp.concatenate(both, axis=1)

    rows_own, rows_near = send_local(*token_parts)
    (rows_own,) = by_z([rows_own])
    (rows_near,) = by_z([rows_near])
    grad_parts = local_rows(combine, out_grad)
    scaled_own, scaled_near = by_z(send_local(*grad_parts))

    base_own = base(rows_own)
    base_near = base(rows_near)
    part_own = added(base_own, rows_own)
    message = part_own.astype(BF16)
    near_extra = moves.column_pair(message)
    part_near = added(base_near, rows_near)
    message = part_near.astype(BF16)
    own_extra = moves.column_pair(message)

    def act(part, extra):
        total = part + extra.astype(F32)
        gate_act, up_act = total[:, :hidden], total[:, hidden:]
        sigmoid_gate = jax.nn.sigmoid(gate_act)
        swish_gate = gate_act * sigmoid_gate
        slope = up_act * sigmoid_gate * (1.0 + gate_act * (1.0 - sigmoid_gate))
        return lax.optimization_barrier(((swish_gate * up_act).astype(BF16), slope, swish_gate))

    act_near, slope_near, swish_near = act(part_near, near_extra)
    out_near = outward([(act_near, 2)])
    act_own, slope_own, swish_own = act(part_own, own_extra)
    out_own = outward([(act_own, 2)])
    (back_near,) = by_z([out_near])
    (back_own,) = by_z([out_own])

    hid_own, hid_near = inward(scaled_own, 2), inward(scaled_near, 2)
    message = jnp.concatenate([hid_near, hid_own]).astype(BF16)
    extra = moves.column_pair(message)
    hid_own = hid_own + extra[: 2 * half].astype(F32)
    hid_near = hid_near + extra[2 * half :].astype(F32)
    gg_near, ug_near = (hid_near * slope_near).astype(BF16), (hid_near * swish_near).astype(BF16)
    gg_own, ug_own = (hid_own * slope_own).astype(BF16), (hid_own * swish_own).astype(BF16)

    rows = jnp.concatenate([rows_own, rows_near])
    scaled = jnp.concatenate([scaled_own, scaled_near])
    activation = jnp.concatenate([act_own, act_near])
    gate_grad = jnp.concatenate([gg_own, gg_near])
    up_grad = jnp.concatenate([ug_own, ug_near])
    first, second = slice(0, quarter_width), slice(quarter_width, half_width)
    term_far = contract(scaled[:, second], activation, 0, 0).astype(BF16)
    arrived_down = moves.weight_pair(term_far)
    grad_near = outward([(gg_near, 0), (ug_near, 1)])
    (grad_near,) = by_z([grad_near])
    gate_far = contract(rows[:, second], gate_grad, 0, 0).astype(BF16)
    arrived_gate = moves.weight_pair(gate_far)
    up_far = contract(rows[:, second], up_grad, 0, 0).astype(BF16)
    arrived_up = moves.weight_pair(up_far)
    grad_own = outward([(gg_own, 0), (ug_own, 1)])
    (grad_own,) = by_z([grad_own])
    moe_out = give_back(combine, back_own, back_near)
    token_grad = give_back_crossed(dispatch, grad_own, grad_near)
    term_down = contract(scaled[:, first], activation, 0, 0) + arrived_down.astype(F32)
    term_down = term_down.astype(BF16)
    own_gate = contract(rows[:, first], gate_grad, 0, 0)
    own_up = contract(rows[:, first], up_grad, 0, 0)
    weight_grad = first_terms(own_gate, arrived_gate, term_down)
    weight_grad = last_term(weight_grad, own_up, arrived_up)
    return moe_out, token_grad, jnp.transpose(weight_grad, (1, 0, 2))[None]


def gathered(tokens, expert_ids, gate_units, expert_weights, out_grad):
    experts = lax.axis_size("expert")
    slots = experts * CAP
    width = tokens.shape[1]
    hidden = expert_weights.shape[3]
    slot = jnp.arange(slots, dtype=jnp.int32)
    dispatch, combine = route_tables(expert_ids, gate_units, slot // CAP, slot % CAP)

    def exchange(rows):
        return lax.all_to_all(
            rows.reshape(experts, CAP, width), "expert", split_axis=0, concat_axis=0, tiled=True
        ).reshape(slots, width)

    slot_rows = exchange(contract(dispatch, tokens, 0, 0).astype(BF16))
    scaled = exchange(contract(combine, out_grad, 0, 0).astype(BF16))
    full = lax.all_gather(expert_weights, ("dp", "fsdp"), axis=1, tiled=True)[0]
    gate_act = contract(slot_rows, full[:, 0], 1, 0)
    up_act = contract(slot_rows, full[:, 1], 1, 0)
    sigmoid_gate = jax.nn.sigmoid(gate_act)
    swish_gate = gate_act * sigmoid_gate
    activation = (swish_gate * up_act).astype(BF16)
    result = contract(activation, full[:, 2], 1, 1).astype(BF16)
    moe_out = contract(combine, exchange(result), 1, 0).astype(BF16)
    hidden_grad = contract(scaled, full[:, 2], 1, 0)
    gate_grad = (
        hidden_grad * up_act * sigmoid_gate * (1.0 + gate_act * (1.0 - sigmoid_gate))
    ).astype(BF16)
    up_grad = (hidden_grad * swish_gate).astype(BF16)
    row_grad = (
        contract(gate_grad, full[:, 0], 1, 1) + contract(up_grad, full[:, 1], 1, 1)
    ).astype(BF16)
    token_grad = contract(dispatch, exchange(row_grad), 1, 0).astype(BF16)
    term = jnp.stack(
        [
            contract(slot_rows, gate_grad, 0, 0),
            contract(slot_rows, up_grad, 0, 0),
            contract(scaled, activation, 0, 0),
        ],
        axis=1,
    ).astype(BF16)
    summed = lax.psum_scatter(term, ("dp", "fsdp"), scatter_dimension=0, tiled=True)
    return moe_out, token_grad, summed.reshape(1, -1, 3, hidden)


def solution(mesh):
    placed = P(ALL, None)
    weights = P("expert", ("dp", "fsdp"), None, None)
    sizes = mesh.shape
    steps = sizes["expert"] // 2
    small = sizes["dp"] == 2 and sizes["fsdp"] == 2 and steps > 1
    small = small and sizes["expert"] % 2 == 0 and steps & (steps - 1) == 0
    return jax.shard_map(
        paired if small else gathered,
        mesh=mesh,
        in_specs=(placed, placed, placed, weights, placed),
        out_specs=(placed, placed, weights),
        check_vma=False,
    )
```
